32 devices in a mesh: prompt: 4 (over y, x), sample: 8 (over z, core).
Axes of the slice: x: 2, y: 2, z: 4, core: 2. Of those that a mesh axis runs over, the one named last changes fastest.
Arguments:
- embeddings: bfloat16 [32, 512, 1024], P(('prompt', 'sample')), parts along dimension 0
- lengths: int32 [32], P(('prompt', 'sample')), parts along dimension 0, may hold values from 32 to 512, as said below
Outputs:
- precision: float32 [32, 8], P(('prompt', 'sample')), parts along dimension 0
- utility: float32 [32], P(('prompt', 'sample')), parts along dimension 0
The draws below stay inside these ranges and needn't reach their ends.
There are 4 independent parts, one for each index of `prompt`. The reference program is written for one: setup_inputs(seed, part) draws one part's arguments, and reference() takes and returns one part's arrays. A program takes and returns all parts, laid end to end along the dimension named above; each array names one. Nothing has to cross between parts.
Inputs may be any that keep to these rules, and one draw needn't show every extreme that they name: `lengths`: some sample of the prompt has exactly 512 tokens.
All inputs are finite; a program needn't handle non-finite values.
Results may differ from the reference program's by a relative error of at most 0.0007.
Values may be sent and summed in bfloat16 or wider, within the bound.
A program may use at most 128 MiB of HBM per device.

```python
import jax
import jax.numpy as jnp
from jax import lax

E = 1024
LEN = 512
SAMPLES = 8


def draw_embeddings(key, part):
    keys = jax.random.split(jax.random.fold_in(key, 11), 4)
    pool = jax.random.normal(keys[0], (256, E), jnp.float32)
    offset = jax.random.randint(keys[1], (SAMPLES, 1), 0, 160)
    concept = offset + jax.random.randint(keys[2], (SAMPLES, LEN), 0, 96)
    centre = jnp.take(pool, concept, axis=0)
    noise = jax.random.normal(keys[3], (SAMPLES, LEN, E), jnp.float32)
    result = centre + 0.6 * noise
    return result.astype(jnp.bfloat16)


def draw_lengths(key, part):
    keys = jax.random.split(jax.random.fold_in(key, 23), 2)
    drawn = jax.random.randint(keys[0], (SAMPLES,), max(1, LEN // 16), LEN + 1)
    chosen = jax.random.randint(keys[1], (), 0, SAMPLES)
    return jnp.where(jnp.arange(SAMPLES) == chosen, LEN, drawn).astype(jnp.int32)


def setup_inputs(seed: int = 0, part: int = 0) -> dict:
    arg_keys = jax.random.split(jax.random.key(seed), 3)
    part_splits = jax.random.split(jax.random.fold_in(arg_keys[2], part), 3)
    return {
        "embeddings": draw_embeddings(jax.random.fold_in(jax.random.fold_in(arg_keys[2], part), 71), part),
        "lengths": draw_lengths(jax.random.fold_in(jax.random.fold_in(arg_keys[2], part), 71), part),
    }


def reference(embeddings, lengths):
    values = embeddings.astype(jnp.float32)
    unit = (values / jnp.sqrt(lax.optimization_barrier(jnp.sum(values * values, axis=2, keepdims=True)) + 1e-06)).astype(jnp.bfloat16)
    flat = unit.reshape(SAMPLES * LEN, E)
    places = jnp.arange(LEN, dtype=jnp.int32)
    valid = places[None, :] < lengths[:, None]

    def one_row(items):
        own, own_len = items
        similar = jnp.dot(own, flat.T, preferred_element_type=jnp.float32).reshape(LEN, SAMPLES, LEN)
        masked = jnp.where(valid[None, :, :], similar, jnp.float32(-4.0))
        best = lax.optimization_barrier(jnp.max(masked, axis=2))
        keep = places[:, None] < own_len
        return lax.optimization_barrier(jnp.sum(jnp.where(keep, best, jnp.float32(0.0)), axis=0)) / own_len.astype(jnp.float32)
    precision = lax.map(one_row, (unit, lengths))
    both = precision + precision.T
    offdiag = jnp.arange(SAMPLES)[:, None] != jnp.arange(SAMPLES)[None, :]
    utility = lax.optimization_barrier(jnp.sum(jnp.where(offdiag, both, jnp.float32(0.0)), axis=1)) / jnp.float32(2 * (SAMPLES - 1))
    return (precision, utility)
```

```python
import functools

import jax
import jax.numpy as jnp
from jax import lax
from jax.experimental import pallas as pl
from jax.experimental.pallas import tpu as pltpu
from jax.sharding import PartitionSpec as P

MESH = pl.DeviceIdType.MESH
T = 128
FIRST = (32, 32, 64)


def pieces_of(length):
    sizes = list(FIRST) + [T] * (length // T - sum(FIRST) // T)
    return [(sum(sizes[:i]), n) for i, n in enumerate(sizes)]


def kernel(chips, slots, emb_ref, len_ref, out_ref, stage, own, left, right, relay, count, lens, rows, cols, pair, res,
           load, main_out, side_out, own_out, own_in, left_in, late_in, relay_in, relay_out, right_in, right_out,
           lens_out, lens_in, res_out, res_in):
    p, s = lax.axis_index("prompt"), lax.axis_index("sample")
    x, y, z, c = p % 2, p // 2, s // 2, s % 2
    flip = (x + y) % 2
    v = jnp.where(flip == 0, z, chips - 1 - z)
    across = jnp.where(c == 0, p + 1 - 2 * x, p + 2 - 4 * y)
    length, width = own.shape[1:]
    chunks = length // T
    halves = length // (2 * T)
    pieces = pieces_of(length)
    sib = 2 * z + 1 - c
    is_far, is_near, is_hub, is_end = v == 0, v == 1, v == 2, v == 3
    f32 = jnp.float32

    def sample(place, core):
        return 2 * jnp.where(flip == 0, place, chips - 1 - place) + core

    def at(prompt, who):
        return {"prompt": prompt, "sample": who}

    def copy(src, dst, out_sem, in_sem, where):
        return pltpu.make_async_remote_copy(
            src_ref=src, dst_ref=dst, send_sem=out_sem, recv_sem=in_sem,
            device_id=where, device_id_type=MESH)

    def chunk(k):
        return pl.ds(k * T, T)

    far, near, hub, end = (sample(i, c) for i in range(chips))
    hub_other, end_other = sample(2, 1 - c), sample(3, 1 - c)
    twin = at(across, 2 * (chips - 1 - z) + c)

    barrier = pltpu.get_barrier_semaphore()

    def greet(where):
        pl.semaphore_signal(barrier, inc=1, device_id=where, device_id_type=MESH)

    greet(at(p, sib))

    @pl.when(is_far)
    def _():
        greet(at(p, near))
        greet(at(p, hub))

    @pl.when(is_near)
    def _():
        greet(at(p, far))
        greet(at(p, hub))

    @pl.when(is_hub)
    def _():
        greet(at(across, s))
        greet(at(p, near))
        greet(at(p, far))
        greet(at(p, end))
        greet(at(p, end_other))
        greet(twin)

    @pl.when(is_end)
    def _():
        greet(at(p, hub))
        greet(at(p, hub_other))

    def fetch(k):
        return pltpu.make_async_copy(emb_ref.at[0, chunk(k)], stage.at[k], load.at[k])

    fetch_len = pltpu.make_async_copy(len_ref, count, load.at[chunks])
    fetch_len.start()
    for k in range(chunks):
        fetch(k).start()
    fetch_len.wait()
    mine = count[0]
    lens[s] = jnp.full(lens.shape[1:], mine, jnp.int32)
    token = lax.broadcasted_iota(jnp.int32, (T, 1), 0)
    first = None
    for k in range(chunks):
        fetch(k).wait()
        values = stage[k].astype(f32)
        unit = values * (1.0 / jnp.sqrt(jnp.sum(values * values, axis=1, keepdims=True) + 1e-06))
        first = unit[0:1] if first is None else first
        own[0, k * T:(k + 1) * T] = jnp.where(token + k * T < mine, unit, first).astype(own.dtype)

    def straight(k):
        return copy(own.at[0, chunk(k)], left.at[k, 0], main_out.at[k], left_in.at[k], at(p, hub))

    def inward(k):
        return copy(own.at[0, chunk(k)], right.at[k, 0], main_out.at[k], right_in.at[0, k], at(p, hub))

    def detour(i):
        lo, n = pieces[i]
        return copy(own.at[0, pl.ds(lo, n)], relay.at[pl.ds(lo, n)], main_out.at[i], relay_in.at[i], at(across, s))

    def hand_on(i):
        lo, n = pieces[i]
        return copy(relay.at[pl.ds(lo, n)], left.at[lo // T, 1, pl.ds(lo % T, n)], relay_out.at[i], late_in.at[i], twin)

    def outward(k, who):
        return copy(own.at[0, chunk(k)], left.at[k, 0], side_out.at[k], left_in.at[k], at(p, who))

    def to_side(k):
        return copy(right.at[k, 0], right.at[k, 1], right_out.at[k], right_in.at[1, k], at(p, sib))

    def tell(i, who):
        return copy(lens.at[s], lens.at[s], lens_out.at[i], lens_in.at[s], at(p, who))

    def told(who):
        copy(lens.at[who], lens.at[who], lens_out.at[0], lens_in.at[who], at(p, sib)).wait_recv()

    def report(i, slot, who):
        return copy(res.at[0], res.at[slot], res_out.at[i], res_in.at[slot], at(p, who))

    share = copy(own.at[0], own.at[1], own_out, own_in, at(p, sib))

    @pl.when(is_far)
    def _():
        pl.semaphore_wait(barrier, 3)
        for k in range(chunks):
            straight(k).start()
        tell(1, hub).start()

    @pl.when(is_near)
    def _():
        pl.semaphore_wait(barrier, 4)
        for i in range(len(pieces)):
            detour(i).start()
        for k in range(chunks):
            outward(k, far).start()
        tell(1, hub).start()
        tell(2, far).start()

    @pl.when(is_hub)
    def _():
        pl.semaphore_wait(barrier, 6)
        for k in range(chunks):
            outward(k, end).start()
        tell(1, end).start()

    @pl.when(is_end)
    def _():
        pl.semaphore_wait(barrier, 3)
        for k in range(chunks):
            inward(k).start()
        tell(1, hub).start()
        tell(2, hub_other).start()

    share.start()
    tell(0, sib).start()

    def pass_on(i):
        hand_wait = copy(relay.at[pl.ds(*pieces[i])], relay.at[pl.ds(*pieces[i])], relay_out.at[i], relay_in.at[i], twin)
        hand_wait.wait_recv()
        hand_on(i).start()

    @pl.when(is_hub)
    def _():
        for i in range(len(FIRST) - 1):
            pass_on(i)

    def dot(a, b):
        return lax.dot_general(a, b, (((1,), (1,)), ((), ())), preferred_element_type=f32)

    def fold(old, new):
        return new if old is None else jnp.maximum(old, new)

    def plus(old, new):
        return new if old is None else old + new

    def down(part):
        return jnp.max(part.reshape(part.shape[0] // 8, 8, part.shape[1]), axis=0)

    def length_of(who):
        return lens[who, 0:1, 0:1]

    def row_sum(best, start, who):
        top = jnp.max(best, axis=1, keepdims=True)
        place = lax.broadcasted_iota(jnp.int32, top.shape, 0) + start
        kept = jnp.where(place < length_of(who), top, f32(0.0))
        return jnp.sum(kept.reshape(top.shape[0] // 8, 8, 1), axis=0)

    def col_sum(best, start, who):
        top = jnp.max(best, axis=0, keepdims=True)
        place = lax.broadcasted_iota(jnp.int32, top.shape, 1) + start
        return jnp.where(place < length_of(who), top, f32(0.0))

    high = lax.broadcasted_iota(jnp.int32, (slots, T), 0)
    wide = lax.broadcasted_iota(jnp.int32, (slots, T), 1)

    def put(table, of, against, total):
        value = jnp.sum(jnp.sum(total, axis=0, keepdims=True), axis=1, keepdims=True)
        value = value / length_of(of).astype(f32)
        return jnp.where((high == of) & (wide == against), value, table)

    ours = [s, sib]
    share.wait_recv()
    told(sib)
    by_row = [None] * halves
    by_col = [None, None]
    for h in range(halves):
        y_side = own[0, 2 * T * h:2 * T * (h + 1)]
        best = [None, None]
        for b in range(2):
            for g in range(halves):
                part = dot(own[b, 2 * T * g:2 * T * (g + 1)], y_side)
                best[b] = fold(best[b], down(part))
                if b == 1:
                    by_row[g] = fold(by_row[g], jnp.maximum(part[:, :T], part[:, T:]))
        for b in range(2):
            by_col[b] = plus(by_col[b], col_sum(best[b], 2 * T * h, s))
    table = jnp.zeros((slots, T), f32)
    for b in range(2):
        table = put(table, s, ours[b], by_col[b])
    total = None
    for g in range(halves):
        total = plus(total, row_sum(by_row[g], 2 * T * g, sib))
    pair[...] = put(table, sib, s, total)

    def align(ids, others, ready, steps):
        n = len(ids)
        sums = {}
        for k in range(chunks):
            last = k == chunks - 1
            steps(k)

            def meet(part, r, new, segments):
                parts = [part[:, a * T:(a + 1) * T] for a in range(n)]
                for a in range(n):
                    best = parts[a] if new else jnp.maximum(rows[r, :, a * T:(a + 1) * T], parts[a])
                    if not last:
                        rows[r, :, a * T:(a + 1) * T] = best
                        continue
                    for lo, size, start, who, key in segments:
                        add = row_sum(best[lo:lo + size], start, who)
                        sums[key, a] = plus(sums.get((key, a)), add)

            if others:
                x_side = right[k].reshape(2 * T, width)
                r = 2 * halves + k
                for j in range(k):
                    part = dot(x_side, left[j].reshape(2 * T, width))
                    for b in range(2):
                        cols[j, 2 + b] = jnp.maximum(cols[j, 2 + b], down(part[b * T:(b + 1) * T]))
                    rows[r] = part if j == 0 else jnp.maximum(rows[r], part)
            ready(k)
            y_side = left[k, :n].reshape(n * T, width)
            best = [None] * 4
            for b in range(2):
                for h in range(halves):
                    part = dot(own[b, 2 * T * h:2 * T * (h + 1)], y_side)
                    best[b] = fold(best[b], down(part))
                    meet(part, b * halves + h, k == 0, [(0, 2 * T, 2 * T * h, ours[b], ours_key(b))])
            if others:
                for j in range(k + 1):
                    part = dot(right[j].reshape(2 * T, width), y_side)
                    for b in range(2):
                        best[2 + b] = fold(best[2 + b], down(part[b * T:(b + 1) * T]))
                    meet(part, 2 * halves + j, k == 0,
                         [(b * T, T, j * T, others[b], 2 + b) for b in range(2)])
            for b in range(4 if others else 2):
                cols[k, b, :, :n * T] = best[b]
        table = jnp.zeros((slots, T), f32)
        whose = ours + list(others)
        for b in range(len(whose)):
            for a in range(n):
                across_sum = None
                for k in range(chunks):
                    across_sum = plus(across_sum, col_sum(cols[k, b, :, a * T:(a + 1) * T], k * T, ids[a]))
                table = put(table, ids[a], whose[b], across_sum)
                table = put(table, whose[b], ids[a], sums[b, a])
        res[0] = table

    def ours_key(b):
        return b

    def arrived(k):
        copy(left.at[k, 0], left.at[k, 0], main_out.at[k], left_in.at[k], at(p, hub)).wait_recv()

    @pl.when(is_hub)
    def _():
        ids = [far, near]
        others = [end, end_other]

        def steps(k):
            if k == 0:
                for who in ids + others:
                    told(who)
                for i in range(len(FIRST) - 1, len(FIRST) + 1):
                    pass_on(i)
            elif len(FIRST) + k < len(pieces):
                pass_on(len(FIRST) + k)
            copy(right.at[k, 0], right.at[k, 0], right_out.at[k], right_in.at[0, k], at(p, sib)).wait_recv()
            to_side(k).start()
            to_side(k).wait_recv()

        def ready(k):
            arrived(k)
            for i, (lo, n) in enumerate(pieces):
                if lo // T == k:
                    hand_on(i).wait_recv()

        align(ids, others, ready, steps)
        report(0, 1, sib).start()
        report(1, 2, far).start()
        report(2, 2, near).start()
        report(3, 2, end).start()
        report(4, 3, end_other).start()

    @pl.when(is_far | is_end)
    def _():
        who = jnp.where(is_far, near, hub)

        def steps(k):
            if k == 0:
                told(who)

        align([who], [], arrived, steps)
        report(0, 1, sib).start()
        report(1, 3, who).start()

    def reported(slot):
        copy(res.at[slot], res.at[slot], res_out.at[0], res_in.at[slot], at(p, sib)).wait_recv()

    @pl.when(is_near)
    def _():
        res[0] = jnp.zeros(res.shape[1:], f32)
        res[1] = jnp.zeros(res.shape[1:], f32)
        for i in range(len(pieces)):
            detour(i).wait_send()
        for k in range(chunks):
            outward(k, far).wait_send()
        tell(1, hub).wait_send()
        tell(2, far).wait_send()
        reported(3)
        reported(2)

    @pl.when(is_far)
    def _():
        res[3] = jnp.zeros(res.shape[1:], f32)
        for k in range(chunks):
            straight(k).wait_send()
        tell(1, hub).wait_send()
        report(0, 1, sib).wait_send()
        report(1, 3, near).wait_send()
        reported(1)
        reported(2)

    @pl.when(is_hub)
    def _():
        res[2] = jnp.zeros(res.shape[1:], f32)
        for k in range(chunks):
            outward(k, end).wait_send()
            to_side(k).wait_send()
        for i in range(len(pieces)):
            hand_on(i).wait_send()
        tell(1, end).wait_send()
        reported(3)
        reported(1)

    @pl.when(is_end)
    def _():
        for k in range(chunks):
            inward(k).wait_send()
        tell(1, hub).wait_send()
        tell(2, hub_other).wait_send()
        report(0, 1, sib).wait_send()
        report(1, 3, hub).wait_send()
        for slot in range(1, 4):
            reported(slot)

    whole = pair[...] + res[0] + res[1] + res[2] + res[3]
    row = jnp.sum(jnp.where(high == s, whole, f32(0.0)), axis=0, keepdims=True)
    mine_too = ((high == s) | (wide == s)) & (high != wide)
    both = jnp.sum(jnp.where(mine_too, whole, f32(0.0)), axis=0, keepdims=True)
    score = jnp.sum(both, axis=1, keepdims=True) / f32(2 * (slots - 1))
    out_ref[...] = jnp.where(high == 0, row, score)
    share.wait_send()
    tell(0, sib).wait_send()

    @pl.when(is_hub)
    def _():
        report(0, 1, sib).wait_send()
        report(1, 2, far).wait_send()
        report(2, 2, near).wait_send()
        report(3, 2, end).wait_send()
        report(4, 3, end_other).wait_send()


def finish(found_ref, precision_ref, utility_ref):
    precision_ref[...] = found_ref[0:1, :precision_ref.shape[1]]
    utility_ref[...] = found_ref[1:2, 0:1]


def fused(slots, embeddings, lengths):
    length, width = embeddings.shape[1:]
    chunks = length // T
    count = len(pieces_of(length))
    dma = pltpu.SemaphoreType.DMA
    vmem = pl.BlockSpec(memory_space=pltpu.VMEM)
    away = pl.BlockSpec(memory_space=pl.ANY)
    found = pl.pallas_call(
        functools.partial(kernel, slots // 2, slots),
        out_shape=jax.ShapeDtypeStruct((slots, T), jnp.float32),
        in_specs=[away, away],
        out_specs=vmem,
        scratch_shapes=[
            pltpu.VMEM((chunks, T, width), jnp.bfloat16),
            pltpu.VMEM((2, length, width), jnp.bfloat16),
            pltpu.VMEM((chunks, 2, T, width), jnp.bfloat16),
            pltpu.VMEM((chunks, 2, T, width), jnp.bfloat16),
            pltpu.VMEM((length, width), jnp.bfloat16),
            pltpu.SMEM((1,), jnp.int32),
            pltpu.VMEM((slots, 8, T), jnp.int32),
            pltpu.VMEM((2 * chunks, 2 * T, 2 * T), jnp.float32),
            pltpu.VMEM((chunks, 4, 8, 2 * T), jnp.float32),
            pltpu.VMEM((slots, T), jnp.float32),
            pltpu.VMEM((4, slots, T), jnp.float32),
            dma((chunks + 1,)), dma((count,)), dma((chunks,)), dma(()), dma(()), dma((chunks,)), dma((count,)),
            dma((count,)), dma((count,)), dma((2, chunks)), dma((chunks,)),
            dma((3,)), dma((slots,)), dma((5,)), dma((4,)),
        ],
        compiler_params=pltpu.CompilerParams(collective_id=0, has_side_effects=True),
    )(embeddings, lengths)
    precision, utility = pl.pallas_call(
        finish,
        out_shape=(jax.ShapeDtypeStruct((1, slots), jnp.float32), jax.ShapeDtypeStruct((1, 1), jnp.float32)),
        in_specs=[vmem],
        out_specs=(vmem, vmem),
    )(found)
    return precision, utility[:, 0]


def tile_pairs(own, own_len, other, other_len):
    similar = jnp.einsum("aie,bje->abij", own, other, preferred_element_type=jnp.float32)
    places = jnp.arange(own.shape[1], dtype=jnp.int32)
    own_ok = places[None, :] < own_len[:, None]
    other_ok = places[None, :] < other_len[:, None]
    masked = jnp.where(other_ok[None, :, None, :], similar, jnp.float32(-4.0))
    best_row = jnp.max(masked, axis=3)
    forward = jnp.sum(jnp.where(own_ok[:, None, :], best_row, jnp.float32(0.0)), axis=2)
    forward = forward / own_len[:, None].astype(jnp.float32)
    masked_col = jnp.where(own_ok[:, None, :, None], similar, jnp.float32(-4.0))
    best_col = jnp.max(masked_col, axis=2)
    backward = jnp.sum(jnp.where(other_ok[None, :, :], best_col, jnp.float32(0.0)), axis=2)
    backward = backward / other_len[None, :].astype(jnp.float32)
    return (forward, backward)


def body(embeddings, lengths):
    values = embeddings.astype(jnp.float32)
    unit = (values / jnp.sqrt(jnp.sum(values * values, axis=2, keepdims=True) + 1e-06)).astype(
        jnp.bfloat16
    )
    devices = lax.axis_size("sample")
    here = lax.axis_index("sample")
    per_dev = unit.shape[0]
    total = per_dev * devices
    base = here * per_dev
    piece = lax.all_gather(unit, "sample", axis=0, tiled=True)
    piece_len = lax.all_gather(lengths, "sample", axis=0, tiled=True)
    ahead, behind = tile_pairs(unit, lengths, piece, piece_len)
    own_index = base + jnp.arange(per_dev, dtype=jnp.int32)
    offdiag = jnp.arange(total, dtype=jnp.int32)[None, :] != own_index[:, None]
    utility = jnp.sum(jnp.where(offdiag, ahead + behind, jnp.float32(0.0)), axis=1)
    utility = utility / jnp.float32(2 * (total - 1))
    return (ahead, utility)


def solution(mesh):
    in_specs = (P(("prompt", "sample"), None, None), P(("prompt", "sample")))
    out_specs = (P(("prompt", "sample"), None), P(("prompt", "sample")))

    def run(embeddings, lengths):
        slots = mesh.shape["sample"]
        if mesh.shape["prompt"] == 4 and slots == 8 and embeddings.shape[0] == 1 and embeddings.shape[1] % (2 * T) == 0:
            return fused(slots, embeddings, lengths)
        return body(embeddings, lengths)

    return jax.shard_map(run, mesh=mesh, in_specs=in_specs, out_specs=out_specs, check_vma=False)
```

```python
import functools

import jax
import jax.numpy as jnp
from jax import lax
from jax.experimental import pallas as pl
from jax.experimental.pallas import tpu as pltpu
from jax.sharding import PartitionSpec as P

MESH = pl.DeviceIdType.MESH
T = 128
PIECE = 64
FIRST = (32, 32)
FINAL = (32, 32)
AHEAD = 2
HOP = 2
WINDOW = 128


def pieces_of(length):
    sizes = list(FIRST) + [PIECE] * (length // PIECE - 2) + list(FINAL)
    return [(sum(sizes[:i]), n) for i, n in enumerate(sizes)]


def kernel(chips, slots, emb_ref, len_ref, out_ref, stage, own, left, right, relay, number, lens, rows, cols, pair, res,
           load, main_out, side_out, own_out, own_in, left_in, late_in, relay_in, relay_out, right_in, right_out,
           lens_out, lens_in, res_out, res_in):
    p, s = lax.axis_index("prompt"), lax.axis_index("sample")
    x, y, z, c = p % 2, p // 2, s // 2, s % 2
    flip = (x + y) % 2
    v = jnp.where(flip == 0, z, chips - 1 - z)
    across = jnp.where(c == 0, p + 1 - 2 * x, p + 2 - 4 * y)
    length, width = own.shape[1:]
    chunks = length // T
    halves = length // (2 * T)
    pieces = pieces_of(length)
    count = length // PIECE
    per = T // PIECE
    sib = 2 * z + 1 - c
    is_far, is_near, is_hub, is_end = v == 0, v == 1, v == 2, v == 3
    f32 = jnp.float32

    def sample(place, core):
        return 2 * jnp.where(flip == 0, place, chips - 1 - place) + core

    def at(prompt, who):
        return {"prompt": prompt, "sample": who}

    def copy(src, dst, out_sem, in_sem, where):
        return pltpu.make_async_remote_copy(
            src_ref=src, dst_ref=dst, send_sem=out_sem, recv_sem=in_sem,
            device_id=where, device_id_type=MESH)

    def chunk(k):
        return pl.ds(k * T, T)

    far, near, hub, end = (sample(i, c) for i in range(chips))
    hub_other, end_other = sample(2, 1 - c), sample(3, 1 - c)
    twin = at(across, 2 * (chips - 1 - z) + c)

    barrier = pltpu.get_barrier_semaphore()

    def greet(where):
        pl.semaphore_signal(barrier, inc=1, device_id=where, device_id_type=MESH)

    greet(at(p, sib))

    @pl.when(is_far)
    def _():
        greet(at(p, near))
        greet(at(p, hub))

    @pl.when(is_near)
    def _():
        greet(at(p, far))
        greet(at(p, hub))

    @pl.when(is_hub)
    def _():
        greet(at(across, s))
        greet(at(p, near))
        greet(at(p, far))
        greet(at(p, end))
        greet(at(p, end_other))
        greet(twin)

    @pl.when(is_end)
    def _():
        greet(at(p, hub))
        greet(at(p, hub_other))

    def fetch(k):
        return pltpu.make_async_copy(emb_ref.at[0, chunk(k)], stage.at[k], load.at[k])

    fetch_len = pltpu.make_async_copy(len_ref, number, load.at[chunks])
    fetch_len.start()
    for k in range(chunks):
        fetch(k).start()
    fetch_len.wait()
    mine = number[0]
    lens[s] = jnp.full(lens.shape[1:], mine, jnp.int32)
    token = lax.broadcasted_iota(jnp.int32, (T, 1), 0)

    def scale(k, first):
        fetch(k).wait()
        values = stage[k].astype(f32)
        unit = values * (1.0 / jnp.sqrt(jnp.sum(values * values, axis=1, keepdims=True) + 1e-06))
        first = unit[0:1] if first is None else first
        own[0, k * T:(k + 1) * T] = jnp.where(token + k * T < mine, unit, first).astype(own.dtype)
        return first

    lead = scale(0, None)

    def bit(m):
        return pl.ds(m * PIECE, PIECE)

    def spot(m):
        return pl.ds(m % per * PIECE, PIECE)

    def straight(m):
        return copy(own.at[0, bit(m)], left.at[m // per, 0, spot(m)], main_out.at[m], left_in.at[m], at(p, hub))

    def inward(m):
        return copy(own.at[0, bit(m)], right.at[m // per, 0, spot(m)], main_out.at[m], right_in.at[0, m], at(p, hub))

    def detour(i):
        lo, n = pieces[i]
        return copy(own.at[0, pl.ds(lo, n)], relay.at[pl.ds(lo, n)], main_out.at[i], relay_in.at[i], at(across, s))

    def hand_on(i):
        lo, n = pieces[i]
        return copy(relay.at[pl.ds(lo, n)], left.at[lo // T, 1, pl.ds(lo % T, n)], relay_out.at[i], late_in.at[i], twin)

    def outward(m, who):
        return copy(own.at[0, bit(m)], left.at[m // per, 0, spot(m)], side_out.at[m], left_in.at[m], at(p, who))

    def to_side(m):
        return copy(right.at[m // per, 0, spot(m)], right.at[m // per, 1, spot(m)], right_out.at[m], right_in.at[1, m],
                    at(p, sib))

    def tell(i, who):
        return copy(lens.at[s], lens.at[s], lens_out.at[i], lens_in.at[s], at(p, who))

    def told(who):
        copy(lens.at[who], lens.at[who], lens_out.at[0], lens_in.at[who], at(p, sib)).wait_recv()

    def report(i, slot, who):
        return copy(res.at[0], res.at[slot], res_out.at[i], res_in.at[slot], at(p, who))

    share = copy(own.at[0], own.at[1], own_out, own_in, at(p, sib))

    def paced(send, lo, hi, ahead):
        for i in range(lo, hi):
            if i >= ahead:
                send(i - ahead).wait_send()
            send(i).start()

    def turns(k):
        if k == 0:
            return [("in", 0), ("in", 1), ("on", 2), ("in", 2)]
        m = per * k + 1
        order = [("on", m), ("in", m), ("on", m + 1), ("on", m + 2), ("in", m + 1)]
        done = [("on", m)] if k > 1 else []
        return [turn for turn in order if turn[1] < count and turn not in done]

    def before(i):
        lo, n = pieces[i]
        gone = [j for j, (start, size) in enumerate(pieces[:i]) if start < lo + n - WINDOW]
        return max(gone) if gone else -1

    def pass_on(m):
        for i, (lo, n) in enumerate(pieces):
            if lo // PIECE == m:
                copy(relay.at[pl.ds(lo, n)], relay.at[pl.ds(lo, n)], relay_out.at[i], relay_in.at[i], twin).wait_recv()
                freed = before(i)
                for j in range(before(i - 1) + 1 if i else 0, freed + 1):
                    hand_on(j).wait_send()
                hand_on(i).start()

    @pl.when(is_far)
    def _():
        pl.semaphore_wait(barrier, 3)
        tell(1, hub).start()
        paced(straight, 0, AHEAD, AHEAD)

    @pl.when(is_near)
    def _():
        pl.semaphore_wait(barrier, 4)
        paced(detour, 0, HOP, HOP)
        tell(1, hub).start()
        tell(2, far).start()

    @pl.when(is_hub)
    def _():
        pl.semaphore_wait(barrier, 6)
        tell(1, end).start()

    @pl.when(is_end)
    def _():
        pl.semaphore_wait(barrier, 3)
        tell(1, hub).start()
        tell(2, hub_other).start()
        paced(inward, 0, AHEAD, AHEAD)

    tell(0, sib).start()
    for k in range(1, chunks):
        scale(k, lead)
    share.start()

    @pl.when(is_near)
    def _():
        for m in range(count):
            outward(m, far).start()
        paced(detour, HOP, len(pieces), HOP)

    @pl.when(is_hub)
    def _():
        for m in range(count):
            outward(m, end).start()
        pass_on(0)
        pass_on(1)

    def dot(a, b):
        return lax.dot_general(a, b, (((1,), (1,)), ((), ())), preferred_element_type=f32)

    def fold(old, new):
        return new if old is None else jnp.maximum(old, new)

    def plus(old, new):
        return new if old is None else old + new

    def down(part):
        return jnp.max(part.reshape(part.shape[0] // 8, 8, part.shape[1]), axis=0)

    def length_of(who):
        return lens[who, 0:1, 0:1]

    def row_sum(best, start, who):
        top = jnp.max(best, axis=1, keepdims=True)
        place = lax.broadcasted_iota(jnp.int32, top.shape, 0) + start
        kept = jnp.where(place < length_of(who), top, f32(0.0))
        return jnp.sum(kept.reshape(top.shape[0] // 8, 8, 1), axis=0)

    def col_sum(best, start, who):
        top = jnp.max(best, axis=0, keepdims=True)
        place = lax.broadcasted_iota(jnp.int32, top.shape, 1) + start
        return jnp.where(place < length_of(who), top, f32(0.0))

    high = lax.broadcasted_iota(jnp.int32, (slots, T), 0)
    wide = lax.broadcasted_iota(jnp.int32, (slots, T), 1)

    def put(table, of, against, total):
        value = jnp.sum(jnp.sum(total, axis=0, keepdims=True), axis=1, keepdims=True)
        value = value / length_of(of).astype(f32)
        return jnp.where((high == of) & (wide == against), value, table)

    ours = [s, sib]
    share.wait_recv()
    told(sib)
    by_row = [None] * halves
    by_col = [None, None]
    for h in range(halves):
        y_side = own[0, 2 * T * h:2 * T * (h + 1)]
        best = [None, None]
        for b in range(2):
            for g in range(halves):
                part = dot(own[b, 2 * T * g:2 * T * (g + 1)], y_side)
                best[b] = fold(best[b], down(part))
                if b == 1:
                    by_row[g] = fold(by_row[g], jnp.maximum(part[:, :T], part[:, T:]))
        for b in range(2):
            by_col[b] = plus(by_col[b], col_sum(best[b], 2 * T * h, s))
    table = jnp.zeros((slots, T), f32)
    for b in range(2):
        table = put(table, s, ours[b], by_col[b])
    total = None
    for g in range(halves):
        total = plus(total, row_sum(by_row[g], 2 * T * g, sib))
    pair[...] = put(table, sib, s, total)

    def align(ids, others, ready, steps):
        n = len(ids)
        sums = {}
        for k in range(chunks):
            last = k == chunks - 1
            steps(k)

            def meet(part, r, new, segments):
                parts = [part[:, a * T:(a + 1) * T] for a in range(n)]
                for a in range(n):
                    best = parts[a] if new else jnp.maximum(rows[r, :, a * T:(a + 1) * T], parts[a])
                    if not last:
                        rows[r, :, a * T:(a + 1) * T] = best
                        continue
                    for lo, size, start, who, key in segments:
                        add = row_sum(best[lo:lo + size], start, who)
                        sums[key, a] = plus(sums.get((key, a)), add)

            if others:
                x_side = right[k].reshape(2 * T, width)
                r = 2 * halves + k
                for j in range(k):
                    part = dot(x_side, left[j].reshape(2 * T, width))
                    for b in range(2):
                        cols[j, 2 + b] = jnp.maximum(cols[j, 2 + b], down(part[b * T:(b + 1) * T]))
                    rows[r] = part if j == 0 else jnp.maximum(rows[r], part)
            ready(k)
            y_side = left[k, :n].reshape(n * T, width)
            best = [None] * 4
            for b in range(2):
                for h in range(halves):
                    part = dot(own[b, 2 * T * h:2 * T * (h + 1)], y_side)
                    best[b] = fold(best[b], down(part))
                    meet(part, b * halves + h, k == 0, [(0, 2 * T, 2 * T * h, ours[b], ours_key(b))])
            if others:
                for j in range(k + 1):
                    part = dot(right[j].reshape(2 * T, width), y_side)
                    for b in range(2):
                        best[2 + b] = fold(best[2 + b], down(part[b * T:(b + 1) * T]))
                    meet(part, 2 * halves + j, k == 0,
                         [(b * T, T, j * T, others[b], 2 + b) for b in range(2)])
            for b in range(4 if others else 2):
                cols[k, b, :, :n * T] = best[b]
        table = jnp.zeros((slots, T), f32)
        whose = ours + list(others)
        for b in range(len(whose)):
            for a in range(n):
                across_sum = None
                for k in range(chunks):
                    across_sum = plus(across_sum, col_sum(cols[k, b, :, a * T:(a + 1) * T], k * T, ids[a]))
                table = put(table, ids[a], whose[b], across_sum)
                table = put(table, whose[b], ids[a], sums[b, a])
        res[0] = table

    def ours_key(b):
        return b

    def arrived(k):
        for m in range(per * k, per * k + per):
            straight(m).wait_recv()

    @pl.when(is_hub)
    def _():
        ids = [far, near]
        others = [end, end_other]

        def steps(k):
            if k == 0:
                for who in ids + others:
                    told(who)
            for kind, m in turns(k):
                if kind == "on":
                    pass_on(m)
                else:
                    inward(m).wait_recv()
                    to_side(m).start()
            for m in range(per * k, per * k + per):
                to_side(m).wait_recv()

        def ready(k):
            arrived(k)
            for i, (lo, n) in enumerate(pieces):
                if lo // T == k:
                    hand_on(i).wait_recv()

        align(ids, others, ready, steps)
        report(0, 1, sib).start()
        report(1, 2, far).start()
        report(2, 2, near).start()
        report(3, 2, end).start()
        report(4, 3, end_other).start()

    @pl.when(is_far | is_end)
    def _():
        who = jnp.where(is_far, near, hub)

        def steps(k):
            if k == 0:
                told(who)

        @pl.when(is_far)
        def _():
            paced(straight, AHEAD, count, AHEAD)

        @pl.when(is_end)
        def _():
            paced(inward, AHEAD, count, AHEAD)

        align([who], [], arrived, steps)
        report(0, 1, sib).start()
        report(1, 3, who).start()

    def reported(slot):
        copy(res.at[slot], res.at[slot], res_out.at[0], res_in.at[slot], at(p, sib)).wait_recv()

    @pl.when(is_near)
    def _():
        res[0] = jnp.zeros(res.shape[1:], f32)
        res[1] = jnp.zeros(res.shape[1:], f32)
        for i in range(len(pieces) - HOP, len(pieces)):
            detour(i).wait_send()
        for m in range(count):
            outward(m, far).wait_send()
        tell(1, hub).wait_send()
        tell(2, far).wait_send()
        reported(3)
        reported(2)

    @pl.when(is_far)
    def _():
        res[3] = jnp.zeros(res.shape[1:], f32)
        for m in range(count - AHEAD, count):
            straight(m).wait_send()
        tell(1, hub).wait_send()
        report(0, 1, sib).wait_send()
        report(1, 3, near).wait_send()
        reported(1)
        reported(2)

    @pl.when(is_hub)
    def _():
        res[2] = jnp.zeros(res.shape[1:], f32)
        for m in range(count):
            outward(m, end).wait_send()
            to_side(m).wait_send()
        for i in range(before(len(pieces) - 1) + 1, len(pieces)):
            hand_on(i).wait_send()
        tell(1, end).wait_send()
        reported(3)
        reported(1)

    @pl.when(is_end)
    def _():
        for m in range(count - AHEAD, count):
            inward(m).wait_send()
        tell(1, hub).wait_send()
        tell(2, hub_other).wait_send()
        report(0, 1, sib).wait_send()
        report(1, 3, hub).wait_send()
        for slot in range(1, 4):
            reported(slot)

    whole = pair[...] + res[0] + res[1] + res[2] + res[3]
    row = jnp.sum(jnp.where(high == s, whole, f32(0.0)), axis=0, keepdims=True)
    mine_too = ((high == s) | (wide == s)) & (high != wide)
    both = jnp.sum(jnp.where(mine_too, whole, f32(0.0)), axis=0, keepdims=True)
    score = jnp.sum(both, axis=1, keepdims=True) / f32(2 * (slots - 1))
    out_ref[...] = jnp.where(high == 0, row, score)
    share.wait_send()
    tell(0, sib).wait_send()

    @pl.when(is_hub)
    def _():
        report(0, 1, sib).wait_send()
        report(1, 2, far).wait_send()
        report(2, 2, near).wait_send()
        report(3, 2, end).wait_send()
        report(4, 3, end_other).wait_send()


def finish(found_ref, precision_ref, utility_ref):
    precision_ref[...] = found_ref[0:1, :precision_ref.shape[1]]
    utility_ref[...] = found_ref[1:2, 0:1]


def fused(slots, embeddings, lengths):
    length, width = embeddings.shape[1:]
    chunks = length // T
    count = len(pieces_of(length))
    many = length // PIECE
    dma = pltpu.SemaphoreType.DMA
    vmem = pl.BlockSpec(memory_space=pltpu.VMEM)
    away = pl.BlockSpec(memory_space=pl.ANY)
    found = pl.pallas_call(
        functools.partial(kernel, slots // 2, slots),
        out_shape=pltpu.VMEM((slots, T), jnp.float32),
        in_specs=[away, pl.BlockSpec(memory_space=pltpu.HBM)],
        out_specs=vmem,
        scratch_shapes=[
            pltpu.VMEM((chunks, T, width), jnp.bfloat16),
            pltpu.VMEM((2, length, width), jnp.bfloat16),
            pltpu.VMEM((chunks, 2, T, width), jnp.bfloat16),
            pltpu.VMEM((chunks, 2, T, width), jnp.bfloat16),
            pltpu.VMEM((length, width), jnp.bfloat16),
            pltpu.SMEM((1,), jnp.int32),
            pltpu.VMEM((slots, 8, T), jnp.int32),
            pltpu.VMEM((2 * chunks, 2 * T, 2 * T), jnp.float32),
            pltpu.VMEM((chunks, 4, 8, 2 * T), jnp.float32),
            pltpu.VMEM((slots, T), jnp.float32),
            pltpu.VMEM((4, slots, T), jnp.float32),
            dma((chunks + 1,)), dma((count,)), dma((many,)), dma(()), dma(()), dma((many,)), dma((count,)),
            dma((count,)), dma((count,)), dma((2, many)), dma((many,)),
            dma((3,)), dma((slots,)), dma((5,)), dma((4,)),
        ],
        compiler_params=pltpu.CompilerParams(collective_id=0, has_side_effects=True),
    )(embeddings, lengths)
    precision, utility = pl.pallas_call(
        finish,
        out_shape=(jax.ShapeDtypeStruct((1, slots), jnp.float32), jax.ShapeDtypeStruct((1, 1), jnp.float32)),
        in_specs=[vmem],
        out_specs=(vmem, vmem),
    )(pltpu.with_memory_space_constraint(found, pltpu.VMEM))
    return precision, utility[:, 0]


def tile_pairs(own, own_len, other, other_len):
    similar = jnp.einsum("aie,bje->abij", own, other, preferred_element_type=jnp.float32)
    places = jnp.arange(own.shape[1], dtype=jnp.int32)
    own_ok = places[None, :] < own_len[:, None]
    other_ok = places[None, :] < other_len[:, None]
    masked = jnp.where(other_ok[None, :, None, :], similar, jnp.float32(-4.0))
    best_row = jnp.max(masked, axis=3)
    forward = jnp.sum(jnp.where(own_ok[:, None, :], best_row, jnp.float32(0.0)), axis=2)
    forward = forward / own_len[:, None].astype(jnp.float32)
    masked_col = jnp.where(own_ok[:, None, :, None], similar, jnp.float32(-4.0))
    best_col = jnp.max(masked_col, axis=2)
    backward = jnp.sum(jnp.where(other_ok[None, :, :], best_col, jnp.float32(0.0)), axis=2)
    backward = backward / other_len[None, :].astype(jnp.float32)
    return (forward, backward)


def body(embeddings, lengths):
    values = embeddings.astype(jnp.float32)
    unit = (values / jnp.sqrt(jnp.sum(values * values, axis=2, keepdims=True) + 1e-06)).astype(
        jnp.bfloat16
    )
    devices = lax.axis_size("sample")
    here = lax.axis_index("sample")
    per_dev = unit.shape[0]
    total = per_dev * devices
    base = here * per_dev
    piece = lax.all_gather(unit, "sample", axis=0, tiled=True)
    piece_len = lax.all_gather(lengths, "sample", axis=0, tiled=True)
    ahead, behind = tile_pairs(unit, lengths, piece, piece_len)
    own_index = base + jnp.arange(per_dev, dtype=jnp.int32)
    offdiag = jnp.arange(total, dtype=jnp.int32)[None, :] != own_index[:, None]
    utility = jnp.sum(jnp.where(offdiag, ahead + behind, jnp.float32(0.0)), axis=1)
    utility = utility / jnp.float32(2 * (total - 1))
    return (ahead, utility)


def solution(mesh):
    in_specs = (P(("prompt", "sample"), None, None), P(("prompt", "sample")))
    out_specs = (P(("prompt", "sample"), None), P(("prompt", "sample")))

    def run(embeddings, lengths):
        slots = mesh.shape["sample"]
        if mesh.shape["prompt"] == 4 and slots == 8 and embeddings.shape[0] == 1 and embeddings.shape[1] % (2 * T) == 0:
            return fused(slots, embeddings, lengths)
        return body(embeddings, lengths)

    return jax.shard_map(run, mesh=mesh, in_specs=in_specs, out_specs=out_specs, check_vma=False)
```

```python
import functools

import jax
import jax.numpy as jnp
from jax import lax
from jax.experimental import pallas as pl
from jax.experimental.pallas import tpu as pltpu
from jax.sharding import PartitionSpec as P

MESH = pl.DeviceIdType.MESH
T = 128
PIECE = 64
FIRST = (32, 32)
FINAL = (16,)
DIRECT = 48
AHEAD = 2
HOP = 2
WINDOW = 128
TURNS = 4


def pieces_of(length):
    middle = length - sum(FIRST) - sum(FINAL) - DIRECT
    sizes = list(FIRST) + [PIECE] * (middle // PIECE) + list(FINAL)
    return [(sum(sizes[:i]), n) for i, n in enumerate(sizes)]


def kernel(chips, slots, emb_ref, len_ref, out_ref, stage, own, left, right, relay, number, lens, rows, cols, pair, res,
           load, main_out, side_out, own_out, own_in, left_in, late_in, relay_in, right_in, side_in, right_out,
           lens_out, lens_in, res_out, res_in):
    p, s = lax.axis_index("prompt"), lax.axis_index("sample")
    x, y, z, c = p % 2, p // 2, s // 2, s % 2
    flip = (x + y) % 2
    v = jnp.where(flip == 0, z, chips - 1 - z)
    across = jnp.where(c == 0, p + 1 - 2 * x, p + 2 - 4 * y)
    length, width = own.shape[1:]
    chunks = length // T
    halves = length // (2 * T)
    pieces = pieces_of(length)
    count = length // PIECE
    per = T // PIECE
    sib = 2 * z + 1 - c
    is_far, is_near, is_hub, is_end = v == 0, v == 1, v == 2, v == 3
    f32 = jnp.float32

    def sample(place, core):
        return 2 * jnp.where(flip == 0, place, chips - 1 - place) + core

    def at(prompt, who):
        return {"prompt": prompt, "sample": who}

    def copy(src, dst, out_sem, in_sem, where):
        return pltpu.make_async_remote_copy(
            src_ref=src, dst_ref=dst, send_sem=out_sem, recv_sem=in_sem,
            device_id=where, device_id_type=MESH)

    def chunk(k):
        return pl.ds(k * T, T)

    far, near, hub, end = (sample(i, c) for i in range(chips))
    hub_other, end_other = sample(2, 1 - c), sample(3, 1 - c)
    twin = at(across, 2 * (chips - 1 - z) + c)

    barrier = pltpu.get_barrier_semaphore()

    def greet(where):
        pl.semaphore_signal(barrier, inc=1, device_id=where, device_id_type=MESH)

    greet(at(p, sib))

    @pl.when(is_far)
    def _():
        greet(at(p, near))
        greet(at(p, hub))

    @pl.when(is_near)
    def _():
        greet(at(p, far))
        greet(at(p, hub))

    @pl.when(is_hub)
    def _():
        greet(at(across, s))
        greet(at(p, near))
        greet(at(p, far))
        greet(at(p, end))
        greet(at(p, end_other))
        greet(twin)

    @pl.when(is_end)
    def _():
        greet(at(p, hub))
        greet(at(p, hub_other))

    def fetch(k):
        return pltpu.make_async_copy(emb_ref.at[0, chunk(k)], stage.at[k], load.at[k])

    fetch_len = pltpu.make_async_copy(len_ref, number, load.at[chunks])
    fetch_len.start()
    for k in range(chunks):
        fetch(k).start()
    fetch_len.wait()
    mine = number[0]
    lens[s] = jnp.full(lens.shape[1:], mine, jnp.int32)
    token = lax.broadcasted_iota(jnp.int32, (T, 1), 0)

    def scale(k, first):
        fetch(k).wait()
        values = stage[k].astype(f32)
        unit = values * (1.0 / jnp.sqrt(jnp.sum(values * values, axis=1, keepdims=True) + 1e-06))
        first = unit[0:1] if first is None else first
        own[0, k * T:(k + 1) * T] = jnp.where(token + k * T < mine, unit, first).astype(own.dtype)
        return first

    lead = scale(0, None)

    def bit(m):
        return pl.ds(m * PIECE, PIECE)

    def spot(m):
        return pl.ds(m % per * PIECE, PIECE)

    def straight(m):
        return copy(own.at[0, bit(m)], left.at[m // per, 0, spot(m)], main_out.at[m % AHEAD], left_in.at[m // per],
                    at(p, hub))

    def inward(m):
        return copy(own.at[0, bit(m)], right.at[m // per, 0, spot(m)], main_out.at[m % AHEAD], right_in.at[m], at(p, hub))

    def detour(i):
        lo, n = pieces[i]
        return copy(own.at[0, pl.ds(lo, n)], relay.at[pl.ds(lo, n)], main_out.at[i % HOP], relay_in.at[i], at(across, s))

    def hand_on(i):
        lo, n = pieces[i]
        return copy(relay.at[pl.ds(lo, n)], left.at[lo // T, 1, pl.ds(lo % T, n)], main_out.at[i % TURNS],
                    late_in.at[lo // T], twin)

    shortcut = copy(own.at[0, pl.ds(length - DIRECT, DIRECT)], left.at[chunks - 1, 1, pl.ds(T - DIRECT, DIRECT)],
                    own_out.at[1], late_in.at[chunks - 1], at(p, hub))

    def outward(k, who):
        return copy(own.at[0, chunk(k)], left.at[k, 0], side_out, left_in.at[k], at(p, who))

    def to_side(m):
        return copy(right.at[m // per, 0, spot(m)], right.at[m // per, 1, spot(m)], right_out, side_in.at[m // per],
                    at(p, sib))

    def tell(i, who):
        return copy(lens.at[s], lens.at[s], lens_out, lens_in.at[i], at(p, who))

    def told(i, who):
        copy(lens.at[who], lens.at[who], lens_out, lens_in.at[i], at(p, sib)).wait_recv()

    def all_sent(sem):
        copy(own.at[0], own.at[0], sem, sem, at(p, sib)).wait_send()

    def small_sent(sem, n):
        copy(lens.at[pl.ds(0, n)], lens.at[pl.ds(0, n)], sem, sem, at(p, sib)).wait_send()

    def report(slot, who):
        return copy(res.at[0], res.at[slot], res_out, res_in.at[slot], at(p, who))

    share = copy(own.at[0], own.at[1], own_out.at[0], own_in, at(p, sib))

    def paced(send, lo, hi, ahead):
        for i in range(lo, hi):
            if i >= ahead:
                send(i - ahead).wait_send()
            send(i).start()

    def turns(k):
        if k == 0:
            return [("in", 0), ("in", 1), ("on", 2), ("in", 2)]
        m = per * k + 1
        order = [("on", m), ("in", m), ("on", m + 1), ("on", m + 2), ("in", m + 1)]
        done = [("on", m)] if k > 1 else []
        return [turn for turn in order if turn[1] < count and turn not in done]

    def before(i):
        lo, n = pieces[i]
        gone = [j for j, (start, size) in enumerate(pieces[:i]) if start < lo + n - WINDOW or j <= i - TURNS]
        return max(gone) if gone else -1

    def pass_on(m):
        for i, (lo, n) in enumerate(pieces):
            if lo // PIECE == m:
                copy(relay.at[pl.ds(lo, n)], relay.at[pl.ds(lo, n)], main_out.at[0], relay_in.at[i], twin).wait_recv()
                freed = before(i)
                for j in range(before(i - 1) + 1 if i else 0, freed + 1):
                    hand_on(j).wait_send()
                hand_on(i).start()

    @pl.when(is_far)
    def _():
        pl.semaphore_wait(barrier, 3)
        tell(1, hub).start()
        paced(straight, 0, AHEAD, AHEAD)

    @pl.when(is_near)
    def _():
        pl.semaphore_wait(barrier, 4)
        paced(detour, 0, HOP, HOP)
        tell(2, hub).start()
        tell(1, far).start()

    @pl.when(is_hub)
    def _():
        pl.semaphore_wait(barrier, 6)
        tell(1, end).start()

    @pl.when(is_end)
    def _():
        pl.semaphore_wait(barrier, 3)
        tell(3, hub).start()
        tell(4, hub_other).start()
        paced(inward, 0, AHEAD, AHEAD)

    tell(0, sib).start()
    for k in range(1, chunks):
        scale(k, lead)
    share.start()

    @pl.when(is_near)
    def _():
        for k in range(chunks):
            outward(k, far).start()
        paced(detour, HOP, len(pieces), HOP)
        shortcut.start()

    @pl.when(is_hub)
    def _():
        for k in range(chunks):
            outward(k, end).start()
        pass_on(0)
        pass_on(1)

    def dot(a, b):
        return lax.dot_general(a, b, (((1,), (1,)), ((), ())), preferred_element_type=f32)

    def fold(old, new):
        return new if old is None else jnp.maximum(old, new)

    def plus(old, new):
        return new if old is None else old + new

    def down(part):
        return jnp.max(part.reshape(part.shape[0] // 8, 8, part.shape[1]), axis=0)

    def length_of(who):
        return lens[who, 0:1, 0:1]

    def row_sum(best, start, who):
        top = jnp.max(best, axis=1, keepdims=True)
        place = lax.broadcasted_iota(jnp.int32, top.shape, 0) + start
        kept = jnp.where(place < length_of(who), top, f32(0.0))
        return jnp.sum(kept.reshape(top.shape[0] // 8, 8, 1), axis=0)

    def col_sum(best, start, who):
        top = jnp.max(best, axis=0, keepdims=True)
        place = lax.broadcasted_iota(jnp.int32, top.shape, 1) + start
        return jnp.where(place < length_of(who), top, f32(0.0))

    high = lax.broadcasted_iota(jnp.int32, (slots, T), 0)
    wide = lax.broadcasted_iota(jnp.int32, (slots, T), 1)

    def put(table, of, against, total):
        value = jnp.sum(jnp.sum(total, axis=0, keepdims=True), axis=1, keepdims=True)
        value = value / length_of(of).astype(f32)
        return jnp.where((high == of) & (wide == against), value, table)

    ours = [s, sib]
    share.wait_recv()
    told(0, sib)
    by_row = [None] * halves
    by_col = [None, None]
    for h in range(halves):
        y_side = own[0, 2 * T * h:2 * T * (h + 1)]
        best = [None, None]
        for b in range(2):
            for g in range(halves):
                part = dot(own[b, 2 * T * g:2 * T * (g + 1)], y_side)
                best[b] = fold(best[b], down(part))
                if b == 1:
                    by_row[g] = fold(by_row[g], jnp.maximum(part[:, :T], part[:, T:]))
        for b in range(2):
            by_col[b] = plus(by_col[b], col_sum(best[b], 2 * T * h, s))
    table = jnp.zeros((slots, T), f32)
    for b in range(2):
        table = put(table, s, ours[b], by_col[b])
    total = None
    for g in range(halves):
        total = plus(total, row_sum(by_row[g], 2 * T * g, sib))
    pair[...] = put(table, sib, s, total)

    def align(ids, others, ready, steps):
        n = len(ids)
        sums = {}
        for k in range(chunks):
            last = k == chunks - 1
            steps(k)

            def meet(part, r, new, segments):
                parts = [part[:, a * T:(a + 1) * T] for a in range(n)]
                for a in range(n):
                    best = parts[a] if new else jnp.maximum(rows[r, :, a * T:(a + 1) * T], parts[a])
                    if not last:
                        rows[r, :, a * T:(a + 1) * T] = best
                        continue
                    for lo, size, start, who, key in segments:
                        add = row_sum(best[lo:lo + size], start, who)
                        sums[key, a] = plus(sums.get((key, a)), add)

            if others:
                x_side = right[k].reshape(2 * T, width)
                r = 2 * halves + k
                for j in range(k):
                    part = dot(x_side, left[j].reshape(2 * T, width))
                    for b in range(2):
                        cols[j, 2 + b] = jnp.maximum(cols[j, 2 + b], down(part[b * T:(b + 1) * T]))
                    rows[r] = part if j == 0 else jnp.maximum(rows[r], part)
            ready(k)
            y_side = left[k, :n].reshape(n * T, width)
            best = [None] * 4
            for b in range(2):
                for h in range(halves):
                    part = dot(own[b, 2 * T * h:2 * T * (h + 1)], y_side)
                    best[b] = fold(best[b], down(part))
                    meet(part, b * halves + h, k == 0, [(0, 2 * T, 2 * T * h, ours[b], ours_key(b))])
            if others:
                for j in range(k + 1):
                    part = dot(right[j].reshape(2 * T, width), y_side)
                    for b in range(2):
                        best[2 + b] = fold(best[2 + b], down(part[b * T:(b + 1) * T]))
                    meet(part, 2 * halves + j, k == 0,
                         [(b * T, T, j * T, others[b], 2 + b) for b in range(2)])
            for b in range(4 if others else 2):
                cols[k, b, :, :n * T] = best[b]
        table = jnp.zeros((slots, T), f32)
        whose = ours + list(others)
        for b in range(len(whose)):
            for a in range(n):
                across_sum = None
                for k in range(chunks):
                    across_sum = plus(across_sum, col_sum(cols[k, b, :, a * T:(a + 1) * T], k * T, ids[a]))
                table = put(table, ids[a], whose[b], across_sum)
                table = put(table, whose[b], ids[a], sums[b, a])
        res[0] = table

    def ours_key(b):
        return b

    def arrived(k):
        copy(left.at[k, 0], left.at[k, 0], side_out, left_in.at[k], at(p, sib)).wait_recv()

    @pl.when(is_hub)
    def _():
        ids = [far, near]
        others = [end, end_other]

        def steps(k):
            if k == 0:
                for i, who in enumerate(ids + others):
                    told(1 + i, who)
            for kind, m in turns(k):
                if kind == "on":
                    pass_on(m)
                else:
                    inward(m).wait_recv()
                    to_side(m).start()
            copy(right.at[k, 1], right.at[k, 1], right_out, side_in.at[k], at(p, sib)).wait_recv()

        def ready(k):
            arrived(k)
            copy(left.at[k, 1], left.at[k, 1], side_out, late_in.at[k], at(p, sib)).wait_recv()

        align(ids, others, ready, steps)
        report(1, sib).start()
        report(2, far).start()
        report(2, near).start()
        report(2, end).start()
        report(3, end_other).start()

    @pl.when(is_far | is_end)
    def _():
        who = jnp.where(is_far, near, hub)

        def steps(k):
            if k == 0:
                told(1, who)

        @pl.when(is_far)
        def _():
            paced(straight, AHEAD, count, AHEAD)

        @pl.when(is_end)
        def _():
            paced(inward, AHEAD, count, AHEAD)

        align([who], [], arrived, steps)
        report(1, sib).start()
        report(3, who).start()

    def reported(slot):
        copy(res.at[slot], res.at[slot], res_out, res_in.at[slot], at(p, sib)).wait_recv()

    @pl.when(is_near)
    def _():
        res[0] = jnp.zeros(res.shape[1:], f32)
        res[1] = jnp.zeros(res.shape[1:], f32)
        for i in range(len(pieces) - HOP, len(pieces)):
            detour(i).wait_send()
        shortcut.wait_send()
        all_sent(side_out)
        small_sent(lens_out, 3)
        reported(3)
        reported(2)

    @pl.when(is_far)
    def _():
        res[3] = jnp.zeros(res.shape[1:], f32)
        for m in range(count - AHEAD, count):
            straight(m).wait_send()
        small_sent(lens_out, 2)
        small_sent(res_out, 2)
        reported(1)
        reported(2)

    @pl.when(is_hub)
    def _():
        res[2] = jnp.zeros(res.shape[1:], f32)
        all_sent(side_out)
        all_sent(right_out)
        for i in range(before(len(pieces) - 1) + 1, len(pieces)):
            hand_on(i).wait_send()
        small_sent(lens_out, 2)
        reported(3)
        reported(1)

    @pl.when(is_end)
    def _():
        for m in range(count - AHEAD, count):
            inward(m).wait_send()
        small_sent(lens_out, 3)
        small_sent(res_out, 2)
        for slot in range(1, 4):
            reported(slot)

    whole = pair[...] + res[0] + res[1] + res[2] + res[3]
    row = jnp.sum(jnp.where(high == s, whole, f32(0.0)), axis=0, keepdims=True)
    mine_too = ((high == s) | (wide == s)) & (high != wide)
    both = jnp.sum(jnp.where(mine_too, whole, f32(0.0)), axis=0, keepdims=True)
    score = jnp.sum(both, axis=1, keepdims=True) / f32(2 * (slots - 1))
    out_ref[...] = jnp.where(high == 0, row, score)
    share.wait_send()

    @pl.when(is_hub)
    def _():
        small_sent(res_out, 5)


def finish(found_ref, precision_ref, utility_ref):
    precision_ref[...] = found_ref[0:1, :precision_ref.shape[1]]
    utility_ref[...] = found_ref[1:2, 0:1]


def fused(slots, embeddings, lengths):
    length, width = embeddings.shape[1:]
    chunks = length // T
    count = len(pieces_of(length))
    many = length // PIECE
    dma = pltpu.SemaphoreType.DMA
    vmem = pl.BlockSpec(memory_space=pltpu.VMEM)
    away = pl.BlockSpec(memory_space=pl.ANY)
    found = pl.pallas_call(
        functools.partial(kernel, slots // 2, slots),
        out_shape=pltpu.VMEM((slots, T), jnp.float32),
        in_specs=[away, pl.BlockSpec(memory_space=pltpu.HBM)],
        out_specs=vmem,
        scratch_shapes=[
            pltpu.VMEM((chunks, T, width), jnp.bfloat16),
            pltpu.VMEM((2, length, width), jnp.bfloat16),
            pltpu.VMEM((chunks, 2, T, width), jnp.bfloat16),
            pltpu.VMEM((chunks, 2, T, width), jnp.bfloat16),
            pltpu.VMEM((length, width), jnp.bfloat16),
            pltpu.SMEM((1,), jnp.int32),
            pltpu.VMEM((slots, 8, T), jnp.int32),
            pltpu.VMEM((2 * chunks, 2 * T, 2 * T), jnp.float32),
            pltpu.VMEM((chunks, 4, 8, 2 * T), jnp.float32),
            pltpu.VMEM((slots, T), jnp.float32),
            pltpu.VMEM((4, slots, T), jnp.float32),
            dma((chunks + 1,)), dma((max(AHEAD, HOP, TURNS),)), dma(()), dma((2,)), dma(()), dma((chunks,)),
            dma((chunks,)), dma((count,)), dma((many,)), dma((chunks,)), dma(()),
            dma(()), dma((5,)), dma(()), dma((4,)),
        ],
        compiler_params=pltpu.CompilerParams(collective_id=0, has_side_effects=True),
    )(embeddings, lengths)
    precision, utility = pl.pallas_call(
        finish,
        out_shape=(jax.ShapeDtypeStruct((1, slots), jnp.float32), jax.ShapeDtypeStruct((1, 1), jnp.float32)),
        in_specs=[vmem],
        out_specs=(vmem, vmem),
    )(pltpu.with_memory_space_constraint(found, pltpu.VMEM))
    return precision, utility[:, 0]


def tile_pairs(own, own_len, other, other_len):
    similar = jnp.einsum("aie,bje->abij", own, other, preferred_element_type=jnp.float32)
    places = jnp.arange(own.shape[1], dtype=jnp.int32)
    own_ok = places[None, :] < own_len[:, None]
    other_ok = places[None, :] < other_len[:, None]
    masked = jnp.where(other_ok[None, :, None, :], similar, jnp.float32(-4.0))
    best_row = jnp.max(masked, axis=3)
    forward = jnp.sum(jnp.where(own_ok[:, None, :], best_row, jnp.float32(0.0)), axis=2)
    forward = forward / own_len[:, None].astype(jnp.float32)
    masked_col = jnp.where(own_ok[:, None, :, None], similar, jnp.float32(-4.0))
    best_col = jnp.max(masked_col, axis=2)
    backward = jnp.sum(jnp.where(other_ok[None, :, :], best_col, jnp.float32(0.0)), axis=2)
    backward = backward / other_len[None, :].astype(jnp.float32)
    return (forward, backward)


def body(embeddings, lengths):
    values = embeddings.astype(jnp.float32)
    unit = (values / jnp.sqrt(jnp.sum(values * values, axis=2, keepdims=True) + 1e-06)).astype(
        jnp.bfloat16
    )
    devices = lax.axis_size("sample")
    here = lax.axis_index("sample")
    per_dev = unit.shape[0]
    total = per_dev * devices
    base = here * per_dev
    piece = lax.all_gather(unit, "sample", axis=0, tiled=True)
    piece_len = lax.all_gather(lengths, "sample", axis=0, tiled=True)
    ahead, behind = tile_pairs(unit, lengths, piece, piece_len)
    own_index = base + jnp.arange(per_dev, dtype=jnp.int32)
    offdiag = jnp.arange(total, dtype=jnp.int32)[None, :] != own_index[:, None]
    utility = jnp.sum(jnp.where(offdiag, ahead + behind, jnp.float32(0.0)), axis=1)
    utility = utility / jnp.float32(2 * (total - 1))
    return (ahead, utility)


def solution(mesh):
    in_specs = (P(("prompt", "sample"), None, None), P(("prompt", "sample")))
    out_specs = (P(("prompt", "sample"), None), P(("prompt", "sample")))

    def run(embeddings, lengths):
        slots = mesh.shape["sample"]
        if mesh.shape["prompt"] == 4 and slots == 8 and embeddings.shape[0] == 1 and embeddings.shape[1] % (2 * T) == 0:
            return fused(slots, embeddings, lengths)
        return body(embeddings, lengths)

    return jax.shard_map(run, mesh=mesh, in_specs=in_specs, out_specs=out_specs, check_vma=False)
```

```python
import functools

import jax
import jax.numpy as jnp
from jax import lax
from jax.experimental import pallas as pl
from jax.experimental.pallas import tpu as pltpu
from jax.sharding import PartitionSpec as P

MESH = pl.DeviceIdType.MESH
T = 128
PIECE = 64
FIRST = (16, 16, 32)
DIRECT = (32, 48)
AHEAD = 2
HOP = 3
WINDOW = 192
TURNS = 4


def pieces_of(length, direct):
    sizes = list(FIRST)
    while sum(sizes) < length - direct:
        sizes.append(min(PIECE, length - direct - sum(sizes)))
    return [(sum(sizes[:i]), n) for i, n in enumerate(sizes)]


def kernel(chips, slots, emb_ref, len_ref, out_ref, stage, own, left, right, relay, number, lens, rows, cols, pair, res,
           load, main_out, side_out, own_out, own_in, left_in, late_in, relay_in, right_in, side_in, right_out,
           lens_out, lens_in, res_out, res_in):
    p, s = lax.axis_index("prompt"), lax.axis_index("sample")
    x, y, z, c = p % 2, p // 2, s // 2, s % 2
    flip = (x + y) % 2
    v = jnp.where(flip == 0, z, chips - 1 - z)
    across = jnp.where(c == 0, p + 1 - 2 * x, p + 2 - 4 * y)
    length, width = own.shape[1:]
    chunks = length // T
    halves = length // (2 * T)
    plans = [pieces_of(length, direct) for direct in DIRECT]
    count = length // PIECE
    per = T // PIECE
    sib = 2 * z + 1 - c
    is_far, is_near, is_hub, is_end = v == 0, v == 1, v == 2, v == 3
    f32 = jnp.float32

    def sample(place, core):
        return 2 * jnp.where(flip == 0, place, chips - 1 - place) + core

    def at(prompt, who):
        return {"prompt": prompt, "sample": who}

    def copy(src, dst, out_sem, in_sem, where):
        return pltpu.make_async_remote_copy(
            src_ref=src, dst_ref=dst, send_sem=out_sem, recv_sem=in_sem,
            device_id=where, device_id_type=MESH)

    def chunk(k):
        return pl.ds(k * T, T)

    far, near, hub, end = (sample(i, c) for i in range(chips))
    hub_other, end_other = sample(2, 1 - c), sample(3, 1 - c)
    twin = at(across, 2 * (chips - 1 - z) + c)

    barrier = pltpu.get_barrier_semaphore()

    def greet(where):
        pl.semaphore_signal(barrier, inc=1, device_id=where, device_id_type=MESH)

    greet(at(p, sib))

    @pl.when(is_far)
    def _():
        greet(at(p, near))
        greet(at(p, hub))

    @pl.when(is_near)
    def _():
        greet(at(p, far))
        greet(at(p, hub))

    @pl.when(is_hub)
    def _():
        greet(at(across, s))
        greet(at(p, near))
        greet(at(p, far))
        greet(at(p, end))
        greet(at(p, end_other))
        greet(twin)

    @pl.when(is_end)
    def _():
        greet(at(p, hub))
        greet(at(p, hub_other))

    def fetch(k):
        return pltpu.make_async_copy(emb_ref.at[0, chunk(k)], stage.at[k], load.at[k])

    fetch_len = pltpu.make_async_copy(len_ref, number, load.at[chunks])
    fetch_len.start()
    for k in range(chunks):
        fetch(k).start()
    fetch_len.wait()
    mine = number[0]
    lens[s] = jnp.full(lens.shape[1:], mine, jnp.int32)
    token = lax.broadcasted_iota(jnp.int32, (T, 1), 0)

    def scale(k, first):
        fetch(k).wait()
        values = stage[k].astype(f32)
        unit = values * (1.0 / jnp.sqrt(jnp.sum(values * values, axis=1, keepdims=True) + 1e-06))
        first = unit[0:1] if first is None else first
        own[0, k * T:(k + 1) * T] = jnp.where(token + k * T < mine, unit, first).astype(own.dtype)
        return first

    lead = scale(0, None)

    def bit(m):
        return pl.ds(m * PIECE, PIECE)

    def spot(m):
        return pl.ds(m % per * PIECE, PIECE)

    def straight(m):
        return copy(own.at[0, bit(m)], left.at[m // per, 0, spot(m)], main_out.at[m % AHEAD], left_in.at[m // per],
                    at(p, hub))

    def inward(m):
        return copy(own.at[0, bit(m)], right.at[m // per, 0, spot(m)], main_out.at[m % AHEAD], right_in.at[m], at(p, hub))

    def detour(f, i):
        lo, n = plans[f][i]
        return copy(own.at[0, pl.ds(lo, n)], relay.at[pl.ds(lo, n)], main_out.at[i % HOP], relay_in.at[i], at(across, s))

    def hand_on(f, i):
        lo, n = plans[f][i]
        return copy(relay.at[pl.ds(lo, n)], left.at[lo // T, 1, pl.ds(lo % T, n)], main_out.at[i % TURNS],
                    late_in.at[lo // T], twin)

    def shortcut(f):
        n = DIRECT[f]
        return copy(own.at[0, pl.ds(length - n, n)], left.at[chunks - 1, 1, pl.ds(T - n, n)],
                    own_out.at[1], late_in.at[chunks - 1], at(p, hub))

    def by_line(which, do):
        for f in range(2):
            pl.when(which == f)(functools.partial(do, f))

    def outward(k, who):
        return copy(own.at[0, chunk(k)], left.at[k, 0], side_out, left_in.at[k], at(p, who))

    def to_side(m):
        return copy(right.at[m // per, 0, spot(m)], right.at[m // per, 1, spot(m)], right_out, side_in.at[m // per],
                    at(p, sib))

    def tell(i, who):
        return copy(lens.at[s], lens.at[s], lens_out, lens_in.at[i], at(p, who))

    def told(i, who):
        copy(lens.at[who], lens.at[who], lens_out, lens_in.at[i], at(p, sib)).wait_recv()

    def all_sent(sem):
        copy(own.at[0], own.at[0], sem, sem, at(p, sib)).wait_send()

    def small_sent(sem, n):
        copy(lens.at[pl.ds(0, n)], lens.at[pl.ds(0, n)], sem, sem, at(p, sib)).wait_send()

    def report(slot, who):
        return copy(res.at[0], res.at[slot], res_out, res_in.at[slot], at(p, who))

    share = copy(own.at[0], own.at[1], own_out.at[0], own_in, at(p, sib))

    def paced(send, lo, hi, ahead):
        for i in range(lo, hi):
            if i >= ahead:
                send(i - ahead).wait_send()
            send(i).start()

    def turns(k):
        return {
            0: [("in", 0), ("in", 1), ("on", 2), ("in", 2), ("on", 3)],
            1: [("in", 3), ("on", 4), ("in", 4), ("on", 5), ("in", 5), ("on", 6)],
            2: [("on", 7), ("in", 6)]}.get(k, [])

    def late_turns(k):
        return {2: [("in", 7)]}.get(k, [])

    def before(f, i):
        lo, n = plans[f][i]
        gone = [j for j, (start, size) in enumerate(plans[f][:i]) if start < lo + n - WINDOW or j <= i - TURNS]
        return max(gone) if gone else -1

    def pass_on(m):
        def do(f):
            for i, (lo, n) in enumerate(plans[f]):
                if lo // PIECE == m:
                    part = relay.at[pl.ds(lo, n)]
                    copy(part, part, main_out.at[0], relay_in.at[i], twin).wait_recv()
                    for j in range(before(f, i - 1) + 1 if i else 0, before(f, i) + 1):
                        hand_on(f, j).wait_send()
                    hand_on(f, i).start()

        by_line(1 - flip, do)

    def passed_on(f):
        for i in range(before(f, len(plans[f]) - 1) + 1, len(plans[f])):
            hand_on(f, i).wait_send()

    def detour_rest(f):
        paced(functools.partial(detour, f), HOP, len(plans[f]), HOP)
        shortcut(f).start()

    def detour_sent(f):
        for i in range(len(plans[f]) - HOP, len(plans[f])):
            detour(f, i).wait_send()
        shortcut(f).wait_send()

    @pl.when(is_far)
    def _():
        pl.semaphore_wait(barrier, 3)
        tell(1, hub).start()
        paced(straight, 0, AHEAD, AHEAD)

    @pl.when(is_near)
    def _():
        pl.semaphore_wait(barrier, 4)
        paced(functools.partial(detour, 0), 0, HOP, HOP)
        tell(2, hub).start()
        tell(1, far).start()

    @pl.when(is_hub)
    def _():
        pl.semaphore_wait(barrier, 6)
        tell(1, end).start()

    @pl.when(is_end)
    def _():
        pl.semaphore_wait(barrier, 3)
        tell(3, hub).start()
        tell(4, hub_other).start()
        paced(inward, 0, AHEAD, AHEAD)

    tell(0, sib).start()
    for k in range(1, chunks):
        scale(k, lead)
    share.start()

    @pl.when(is_near)
    def _():
        for k in range(chunks):
            outward(k, far).start()
        by_line(flip, detour_rest)

    @pl.when(is_hub)
    def _():
        for k in range(chunks):
            outward(k, end).start()
        pass_on(0)
        pass_on(1)

    def dot(a, b):
        return lax.dot_general(a, b, (((1,), (1,)), ((), ())), preferred_element_type=f32)

    def fold(old, new):
        return new if old is None else jnp.maximum(old, new)

    def plus(old, new):
        return new if old is None else old + new

    def down(part):
        return jnp.max(part.reshape(part.shape[0] // 8, 8, part.shape[1]), axis=0)

    def length_of(who):
        return lens[who, 0:1, 0:1]

    def row_sum(best, start, who):
        top = jnp.max(best, axis=1, keepdims=True)
        place = lax.broadcasted_iota(jnp.int32, top.shape, 0) + start
        kept = jnp.where(place < length_of(who), top, f32(0.0))
        return jnp.sum(kept.reshape(top.shape[0] // 8, 8, 1), axis=0)

    def col_sum(best, start, who):
        top = jnp.max(best, axis=0, keepdims=True)
        place = lax.broadcasted_iota(jnp.int32, top.shape, 1) + start
        return jnp.where(place < length_of(who), top, f32(0.0))

    high = lax.broadcasted_iota(jnp.int32, (slots, T), 0)
    wide = lax.broadcasted_iota(jnp.int32, (slots, T), 1)

    def put(table, of, against, total):
        value = jnp.sum(jnp.sum(total, axis=0, keepdims=True), axis=1, keepdims=True)
        value = value / length_of(of).astype(f32)
        return jnp.where((high == of) & (wide == against), value, table)

    ours = [s, sib]
    share.wait_recv()
    told(0, sib)
    by_row = [None] * halves
    by_col = [None, None]
    for h in range(halves):
        y_side = own[0, 2 * T * h:2 * T * (h + 1)]
        best = [None, None]
        for b in range(2):
            for g in range(halves):
                part = dot(own[b, 2 * T * g:2 * T * (g + 1)], y_side)
                best[b] = fold(best[b], down(part))
                if b == 1:
                    by_row[g] = fold(by_row[g], jnp.maximum(part[:, :T], part[:, T:]))
        for b in range(2):
            by_col[b] = plus(by_col[b], col_sum(best[b], 2 * T * h, s))
    table = jnp.zeros((slots, T), f32)
    for b in range(2):
        table = put(table, s, ours[b], by_col[b])
    total = None
    for g in range(halves):
        total = plus(total, row_sum(by_row[g], 2 * T * g, sib))
    pair[...] = put(table, sib, s, total)

    def align(ids, others, ready, steps, halfway=None):
        n = len(ids)
        sums = {}
        for k in range(chunks):
            last = k == chunks - 1
            steps(k)

            def meet(part, r, new, segments):
                parts = [part[:, a * T:(a + 1) * T] for a in range(n)]
                for a in range(n):
                    best = parts[a] if new else jnp.maximum(rows[r, :, a * T:(a + 1) * T], parts[a])
                    if not last:
                        rows[r, :, a * T:(a + 1) * T] = best
                        continue
                    for lo, size, start, who, key in segments:
                        add = row_sum(best[lo:lo + size], start, who)
                        sums[key, a] = plus(sums.get((key, a)), add)

            if others:
                x_side = right[k].reshape(2 * T, width)
                r = 2 * halves + k
                for j in range(k):
                    part = dot(x_side, left[j].reshape(2 * T, width))
                    for b in range(2):
                        cols[j, 2 + b] = jnp.maximum(cols[j, 2 + b], down(part[b * T:(b + 1) * T]))
                    rows[r] = part if j == 0 else jnp.maximum(rows[r], part)
            ready(k)
            y_side = left[k, :n].reshape(n * T, width)
            best = [None] * 4
            for b in range(2):
                for h in range(halves):
                    part = dot(own[b, 2 * T * h:2 * T * (h + 1)], y_side)
                    best[b] = fold(best[b], down(part))
                    meet(part, b * halves + h, k == 0, [(0, 2 * T, 2 * T * h, ours[b], ours_key(b))])
            if others:
                halfway(k)
                for j in range(k + 1):
                    part = dot(right[j].reshape(2 * T, width), y_side)
                    for b in range(2):
                        best[2 + b] = fold(best[2 + b], down(part[b * T:(b + 1) * T]))
                    meet(part, 2 * halves + j, k == 0,
                         [(b * T, T, j * T, others[b], 2 + b) for b in range(2)])
            for b in range(4 if others else 2):
                cols[k, b, :, :n * T] = best[b]
        whose = ours + list(others)
        table = jnp.zeros((slots, T), f32)
        for b in range(len(whose)):
            spread = jnp.zeros((8, T), f32)
            for a in range(n):
                spread = jnp.where(wide == ids[a], sums[b, a], spread)
            line = jnp.sum(spread, axis=0, keepdims=True) / length_of(whose[b]).astype(f32)
            table = jnp.where(high == whose[b], line, table)
        for a in range(n):
            stack = jnp.zeros((slots, T), f32)
            for b in range(len(whose)):
                across_sum = None
                for k in range(chunks):
                    across_sum = plus(across_sum, col_sum(cols[k, b, :, a * T:(a + 1) * T], k * T, ids[a]))
                stack = jnp.where(high == whose[b], across_sum, stack)
            totals = jnp.where(high == wide, jnp.sum(stack, axis=1, keepdims=True), f32(0.0))
            line = jnp.sum(totals, axis=0, keepdims=True) / length_of(ids[a]).astype(f32)
            table = jnp.where(high == ids[a], line, table)
        res[0] = table

    def ours_key(b):
        return b

    def arrived(k):
        copy(left.at[k, 0], left.at[k, 0], side_out, left_in.at[k], at(p, sib)).wait_recv()

    @pl.when(is_hub)
    def _():
        ids = [far, near]
        others = [end, end_other]

        def take(turns):
            for kind, m in turns:
                if kind == "on":
                    pass_on(m)
                else:
                    inward(m).wait_recv()
                    to_side(m).start()

        def halfway(k):
            take(late_turns(k))

        def steps(k):
            if k == 0:
                for i, who in enumerate(ids + others):
                    told(1 + i, who)
            take(turns(k))
            copy(right.at[k, 1], right.at[k, 1], right_out, side_in.at[k], at(p, sib)).wait_recv()

        def ready(k):
            arrived(k)
            copy(left.at[k, 1], left.at[k, 1], side_out, late_in.at[k], at(p, sib)).wait_recv()

        align(ids, others, ready, steps, halfway)
        report(2, far).start()
        report(2, near).start()
        report(2, end).start()
        report(3, end_other).start()
        report(1, sib).start()

    @pl.when(is_far | is_end)
    def _():
        who = jnp.where(is_far, near, hub)

        def steps(k):
            if k == 0:
                told(1, who)

        @pl.when(is_far)
        def _():
            paced(straight, AHEAD, count, AHEAD)

        @pl.when(is_end)
        def _():
            paced(inward, AHEAD, count, AHEAD)

        align([who], [], arrived, steps)
        report(1, sib).start()
        report(3, who).start()

    def reported(slot):
        copy(res.at[slot], res.at[slot], res_out, res_in.at[slot], at(p, sib)).wait_recv()

    @pl.when(is_near)
    def _():
        res[0] = jnp.zeros(res.shape[1:], f32)
        res[1] = jnp.zeros(res.shape[1:], f32)
        by_line(flip, detour_sent)
        all_sent(side_out)
        small_sent(lens_out, 3)
        reported(3)
        reported(2)

    @pl.when(is_far)
    def _():
        res[3] = jnp.zeros(res.shape[1:], f32)
        for m in range(count - AHEAD, count):
            straight(m).wait_send()
        small_sent(lens_out, 2)
        small_sent(res_out, 2)
        reported(1)
        reported(2)

    @pl.when(is_hub)
    def _():
        res[2] = jnp.zeros(res.shape[1:], f32)
        all_sent(side_out)
        all_sent(right_out)
        by_line(1 - flip, passed_on)
        small_sent(lens_out, 2)
        reported(3)
        reported(1)

    @pl.when(is_end)
    def _():
        for m in range(count - AHEAD, count):
            inward(m).wait_send()
        small_sent(lens_out, 3)
        small_sent(res_out, 2)
        for slot in range(1, 4):
            reported(slot)

    whole = pair[...] + res[0] + res[1] + res[2] + res[3]
    row = jnp.sum(jnp.where(high == s, whole, f32(0.0)), axis=0, keepdims=True)
    mine_too = ((high == s) | (wide == s)) & (high != wide)
    both = jnp.sum(jnp.where(mine_too, whole, f32(0.0)), axis=0, keepdims=True)
    score = jnp.sum(both, axis=1, keepdims=True) / f32(2 * (slots - 1))
    out_ref[...] = jnp.where(high == 0, row, score)
    share.wait_send()

    @pl.when(is_hub)
    def _():
        small_sent(res_out, 5)


def finish(found_ref, precision_ref, utility_ref):
    precision_ref[...] = found_ref[0:1, :precision_ref.shape[1]]
    utility_ref[...] = found_ref[1:2, 0:1]


def fused(slots, embeddings, lengths):
    length, width = embeddings.shape[1:]
    chunks = length // T
    count = max(len(pieces_of(length, direct)) for direct in DIRECT)
    many = length // PIECE
    dma = pltpu.SemaphoreType.DMA
    vmem = pl.BlockSpec(memory_space=pltpu.VMEM)
    away = pl.BlockSpec(memory_space=pl.ANY)
    found = pl.pallas_call(
        functools.partial(kernel, slots // 2, slots),
        out_shape=pltpu.VMEM((slots, T), jnp.float32),
        in_specs=[away, pl.BlockSpec(memory_space=pltpu.HBM)],
        out_specs=vmem,
        scratch_shapes=[
            pltpu.VMEM((chunks, T, width), jnp.bfloat16),
            pltpu.VMEM((2, length, width), jnp.bfloat16),
            pltpu.VMEM((chunks, 2, T, width), jnp.bfloat16),
            pltpu.VMEM((chunks, 2, T, width), jnp.bfloat16),
            pltpu.VMEM((length, width), jnp.bfloat16),
            pltpu.SMEM((1,), jnp.int32),
            pltpu.VMEM((slots, 8, T), jnp.int32),
            pltpu.VMEM((2 * chunks, 2 * T, 2 * T), jnp.float32),
            pltpu.VMEM((chunks, 4, 8, 2 * T), jnp.float32),
            pltpu.VMEM((slots, T), jnp.float32),
            pltpu.VMEM((4, slots, T), jnp.float32),
            dma((chunks + 1,)), dma((max(AHEAD, HOP, TURNS),)), dma(()), dma((2,)), dma(()), dma((chunks,)),
            dma((chunks,)), dma((count,)), dma((many,)), dma((chunks,)), dma(()),
            dma(()), dma((5,)), dma(()), dma((4,)),
        ],
        compiler_params=pltpu.CompilerParams(collective_id=0, has_side_effects=True),
    )(embeddings, lengths)
    precision, utility = pl.pallas_call(
        finish,
        out_shape=(jax.ShapeDtypeStruct((1, slots), jnp.float32), jax.ShapeDtypeStruct((1, 1), jnp.float32)),
        in_specs=[vmem],
        out_specs=(vmem, vmem),
    )(pltpu.with_memory_space_constraint(found, pltpu.VMEM))
    return precision, utility[:, 0]


def tile_pairs(own, own_len, other, other_len):
    similar = jnp.einsum("aie,bje->abij", own, other, preferred_element_type=jnp.float32)
    places = jnp.arange(own.shape[1], dtype=jnp.int32)
    own_ok = places[None, :] < own_len[:, None]
    other_ok = places[None, :] < other_len[:, None]
    masked = jnp.where(other_ok[None, :, None, :], similar, jnp.float32(-4.0))
    best_row = jnp.max(masked, axis=3)
    forward = jnp.sum(jnp.where(own_ok[:, None, :], best_row, jnp.float32(0.0)), axis=2)
    forward = forward / own_len[:, None].astype(jnp.float32)
    masked_col = jnp.where(own_ok[:, None, :, None], similar, jnp.float32(-4.0))
    best_col = jnp.max(masked_col, axis=2)
    backward = jnp.sum(jnp.where(other_ok[None, :, :], best_col, jnp.float32(0.0)), axis=2)
    backward = backward / other_len[None, :].astype(jnp.float32)
    return (forward, backward)


def body(embeddings, lengths):
    values = embeddings.astype(jnp.float32)
    unit = (values / jnp.sqrt(jnp.sum(values * values, axis=2, keepdims=True) + 1e-06)).astype(
        jnp.bfloat16
    )
    devices = lax.axis_size("sample")
    here = lax.axis_index("sample")
    per_dev = unit.shape[0]
    total = per_dev * devices
    base = here * per_dev
    piece = lax.all_gather(unit, "sample", axis=0, tiled=True)
    piece_len = lax.all_gather(lengths, "sample", axis=0, tiled=True)
    ahead, behind = tile_pairs(unit, lengths, piece, piece_len)
    own_index = base + jnp.arange(per_dev, dtype=jnp.int32)
    offdiag = jnp.arange(total, dtype=jnp.int32)[None, :] != own_index[:, None]
    utility = jnp.sum(jnp.where(offdiag, ahead + behind, jnp.float32(0.0)), axis=1)
    utility = utility / jnp.float32(2 * (total - 1))
    return (ahead, utility)


def solution(mesh):
    in_specs = (P(("prompt", "sample"), None, None), P(("prompt", "sample")))
    out_specs = (P(("prompt", "sample"), None), P(("prompt", "sample")))

    def run(embeddings, lengths):
        slots = mesh.shape["sample"]
        if mesh.shape["prompt"] == 4 and slots == 8 and embeddings.shape[0] == 1 and embeddings.shape[1] == 4 * T:
            return fused(slots, embeddings, lengths)
        return body(embeddings, lengths)

    return jax.shard_map(run, mesh=mesh, in_specs=in_specs, out_specs=out_specs, check_vma=False)
```

```python
import functools

import jax
import jax.numpy as jnp
from jax import lax
from jax.experimental import pallas as pl
from jax.experimental.pallas import tpu as pltpu
from jax.sharding import PartitionSpec as P

MESH = pl.DeviceIdType.MESH
T = 128
PIECE = 64
FIRST = (16, 16, 32)
DIRECT = (32, 48, 48, 48)
AHEAD = 2
MORE = 3
HOP = (3, 3, 3, 3)
WINDOW = (256, 192, 192, 128)
TURNS = 4


def pieces_of(length, direct):
    sizes = list(FIRST)
    while sum(sizes) < length - direct:
        sizes.append(min(PIECE, length - direct - sum(sizes)))
    return [(sum(sizes[:i]), n) for i, n in enumerate(sizes)]


def kernel(chips, slots, emb_ref, len_ref, out_ref, stage, own, left, right, relay, number, lens, rows, cols, pair, res,
           load, main_out, side_out, own_out, own_in, left_in, late_in, relay_in, right_in, side_in, right_out,
           lens_out, lens_in, res_out, res_in):
    p, s = lax.axis_index("prompt"), lax.axis_index("sample")
    x, y, z, c = p % 2, p // 2, s // 2, s % 2
    flip = (x + y) % 2
    v = jnp.where(flip == 0, z, chips - 1 - z)
    across = jnp.where(c == 0, p + 1 - 2 * x, p + 2 - 4 * y)
    length, width = own.shape[1:]
    chunks = length // T
    halves = length // (2 * T)
    plans = [pieces_of(length, direct) for direct in DIRECT]
    count = length // PIECE
    per = T // PIECE
    sib = 2 * z + 1 - c
    is_far, is_near, is_hub, is_end = v == 0, v == 1, v == 2, v == 3
    f32 = jnp.float32

    def sample(place, core):
        return 2 * jnp.where(flip == 0, place, chips - 1 - place) + core

    def at(prompt, who):
        return {"prompt": prompt, "sample": who}

    def copy(src, dst, out_sem, in_sem, where):
        return pltpu.make_async_remote_copy(
            src_ref=src, dst_ref=dst, send_sem=out_sem, recv_sem=in_sem,
            device_id=where, device_id_type=MESH)

    def chunk(k):
        return pl.ds(k * T, T)

    far, near, hub, end = (sample(i, c) for i in range(chips))
    hub_other, end_other = sample(2, 1 - c), sample(3, 1 - c)
    twin = at(across, 2 * (chips - 1 - z) + c)

    barrier = pltpu.get_barrier_semaphore()

    def greet(where):
        pl.semaphore_signal(barrier, inc=1, device_id=where, device_id_type=MESH)

    greet(at(p, sib))

    @pl.when(is_far)
    def _():
        greet(at(p, near))
        greet(at(p, hub))

    @pl.when(is_near)
    def _():
        greet(at(p, far))
        greet(at(p, hub))

    @pl.when(is_hub)
    def _():
        greet(at(across, s))
        greet(at(p, near))
        greet(at(p, far))
        greet(at(p, end))
        greet(at(p, end_other))
        greet(twin)

    @pl.when(is_end)
    def _():
        greet(at(p, hub))
        greet(at(p, hub_other))

    def fetch(k):
        return pltpu.make_async_copy(emb_ref.at[0, chunk(k)], stage.at[k], load.at[k])

    fetch_len = pltpu.make_async_copy(len_ref, number, load.at[chunks])
    fetch_len.start()
    for k in range(chunks):
        fetch(k).start()
    fetch_len.wait()
    mine = number[0]
    lens[s] = jnp.full(lens.shape[1:], mine, jnp.int32)
    token = lax.broadcasted_iota(jnp.int32, (T, 1), 0)

    def scale(k, first):
        fetch(k).wait()
        values = stage[k].astype(f32)
        unit = values * (1.0 / jnp.sqrt(jnp.sum(values * values, axis=1, keepdims=True) + 1e-06))
        first = unit[0:1] if first is None else first
        own[0, k * T:(k + 1) * T] = jnp.where(token + k * T < mine, unit, first).astype(own.dtype)
        return first

    lead = scale(0, None)

    def bit(m):
        return pl.ds(m * PIECE, PIECE)

    def spot(m):
        return pl.ds(m % per * PIECE, PIECE)

    def straight(m):
        return copy(own.at[0, bit(m)], left.at[m // per, 0, spot(m)], main_out.at[m % TURNS], left_in.at[m // per],
                    at(p, hub))

    def inward(m):
        return copy(own.at[0, bit(m)], right.at[m // per, 0, spot(m)], main_out.at[m % TURNS], right_in.at[m], at(p, hub))

    def detour(f, i):
        lo, n = plans[f][i]
        return copy(own.at[0, pl.ds(lo, n)], relay.at[pl.ds(lo, n)], main_out.at[i % TURNS], relay_in.at[i], at(across, s))

    def hand_on(f, i):
        lo, n = plans[f][i]
        return copy(relay.at[pl.ds(lo, n)], left.at[lo // T, 1, pl.ds(lo % T, n)], main_out.at[i % TURNS],
                    late_in.at[lo // T], twin)

    def shortcut(f):
        n = DIRECT[f]
        return copy(own.at[0, pl.ds(length - n, n)], left.at[chunks - 1, 1, pl.ds(T - n, n)],
                    own_out.at[1], late_in.at[chunks - 1], at(p, hub))

    def by_line(which, do):
        for f in range(len(DIRECT)):
            pl.when(which == f)(functools.partial(do, f))

    def outward(k, who):
        return copy(own.at[0, chunk(k)], left.at[k, 0], side_out, left_in.at[k], at(p, who))

    def to_side(m):
        return copy(right.at[m // per, 0, spot(m)], right.at[m // per, 1, spot(m)], right_out, side_in.at[m // per],
                    at(p, sib))

    def tell(i, who):
        return copy(lens.at[s], lens.at[s], lens_out, lens_in.at[i], at(p, who))

    def told(i, who):
        copy(lens.at[who], lens.at[who], lens_out, lens_in.at[i], at(p, sib)).wait_recv()

    def all_sent(sem):
        copy(own.at[0], own.at[0], sem, sem, at(p, sib)).wait_send()

    def small_sent(sem, n):
        copy(lens.at[pl.ds(0, n)], lens.at[pl.ds(0, n)], sem, sem, at(p, sib)).wait_send()

    def report(slot, who):
        return copy(res.at[0], res.at[slot], res_out, res_in.at[slot], at(p, who))

    share = copy(own.at[0], own.at[1], own_out.at[0], own_in, at(p, sib))

    def paced(send, lo, hi, ahead):
        for i in range(lo, hi):
            if i >= ahead:
                send(i - ahead).wait_send()
            send(i).start()

    def turns(k):
        return {
            0: [("in", 0), ("in", 1), ("on", 2), ("in", 2), ("on", 3)],
            1: [("in", 3), ("on", 4), ("in", 4), ("on", 5), ("in", 5), ("on", 6)],
            2: [("on", 7), ("in", 6)],
            3: [("in", 7)]}[k]

    def before(f, i):
        lo, n = plans[f][i]
        gone = [j for j, (start, size) in enumerate(plans[f][:i]) if start < lo + n - WINDOW[f] or j <= i - TURNS]
        return max(gone) if gone else -1

    def pass_on(m):
        def do(f):
            for i, (lo, n) in enumerate(plans[f]):
                if lo // PIECE == m:
                    part = relay.at[pl.ds(lo, n)]
                    copy(part, part, main_out.at[0], relay_in.at[i], twin).wait_recv()
                    for j in range(before(f, i - 1) + 1 if i else 0, before(f, i) + 1):
                        hand_on(f, j).wait_send()
                    hand_on(f, i).start()

        by_line(across, do)

    def passed_on(f):
        for i in range(before(f, len(plans[f]) - 1) + 1, len(plans[f])):
            hand_on(f, i).wait_send()

    def detour_rest(f):
        paced(functools.partial(detour, f), min(HOP), len(plans[f]), HOP[f])
        shortcut(f).start()

    def detour_sent(f):
        for i in range(len(plans[f]) - HOP[f], len(plans[f])):
            detour(f, i).wait_send()
        shortcut(f).wait_send()

    def done(send, window):
        for m in range(count - window, count):
            send(m).wait_send()

    def by_window(wider, do):
        pl.when(wider)(lambda: do(MORE))
        pl.when(jnp.logical_not(wider))(lambda: do(AHEAD))

    ahead_of = (p == 0) & (c == 0)
    behind = (p == 0) & (c == 1)

    @pl.when(is_far)
    def _():
        pl.semaphore_wait(barrier, 3)
        tell(1, hub).start()
        paced(straight, 0, AHEAD, AHEAD)

    @pl.when(is_near)
    def _():
        pl.semaphore_wait(barrier, 4)
        paced(functools.partial(detour, 0), 0, min(HOP), min(HOP))
        tell(2, hub).start()
        tell(1, far).start()

    @pl.when(is_hub)
    def _():
        pl.semaphore_wait(barrier, 6)
        tell(1, end).start()

    @pl.when(is_end)
    def _():
        pl.semaphore_wait(barrier, 3)
        tell(3, hub).start()
        tell(4, hub_other).start()
        paced(inward, 0, AHEAD, AHEAD)

    tell(0, sib).start()
    for k in range(1, chunks):
        scale(k, lead)
    share.start()

    @pl.when(is_near)
    def _():
        for k in range(chunks):
            outward(k, far).start()
        by_line(p, detour_rest)

    @pl.when(is_hub)
    def _():
        for k in range(chunks):
            outward(k, end).start()
        pass_on(0)
        pass_on(1)

    def dot(a, b):
        return lax.dot_general(a, b, (((1,), (1,)), ((), ())), preferred_element_type=f32)

    def fold(old, new):
        return new if old is None else jnp.maximum(old, new)

    def plus(old, new):
        return new if old is None else old + new

    def down(part):
        return jnp.max(part.reshape(part.shape[0] // 8, 8, part.shape[1]), axis=0)

    def length_of(who):
        return lens[who, 0:1, 0:1]

    def row_sum(best, start, who):
        top = jnp.max(best, axis=1, keepdims=True)
        place = lax.broadcasted_iota(jnp.int32, top.shape, 0) + start
        kept = jnp.where(place < length_of(who), top, f32(0.0))
        return jnp.sum(kept.reshape(top.shape[0] // 8, 8, 1), axis=0)

    def col_sum(best, start, who):
        top = jnp.max(best, axis=0, keepdims=True)
        place = lax.broadcasted_iota(jnp.int32, top.shape, 1) + start
        return jnp.where(place < length_of(who), top, f32(0.0))

    high = lax.broadcasted_iota(jnp.int32, (slots, T), 0)
    wide = lax.broadcasted_iota(jnp.int32, (slots, T), 1)

    def put(table, of, against, total):
        value = jnp.sum(jnp.sum(total, axis=0, keepdims=True), axis=1, keepdims=True)
        value = value / length_of(of).astype(f32)
        return jnp.where((high == of) & (wide == against), value, table)

    ours = [s, sib]
    share.wait_recv()
    told(0, sib)
    by_row = [None] * halves
    by_col = [None, None]
    for h in range(halves):
        y_side = own[0, 2 * T * h:2 * T * (h + 1)]
        best = [None, None]
        for b in range(2):
            for g in range(halves):
                part = dot(own[b, 2 * T * g:2 * T * (g + 1)], y_side)
                best[b] = fold(best[b], down(part))
                if b == 1:
                    by_row[g] = fold(by_row[g], jnp.maximum(part[:, :T], part[:, T:]))
        for b in range(2):
            by_col[b] = plus(by_col[b], col_sum(best[b], 2 * T * h, s))
    table = jnp.zeros((slots, T), f32)
    for b in range(2):
        table = put(table, s, ours[b], by_col[b])
    total = None
    for g in range(halves):
        total = plus(total, row_sum(by_row[g], 2 * T * g, sib))
    pair[...] = put(table, sib, s, total)

    def align(ids, others, ready, steps, landed=None):
        n = len(ids)
        sums = {}
        for k in range(chunks):
            last = k == chunks - 1
            steps(k)

            def meet(part, r, new, segments):
                parts = [part[:, a * T:(a + 1) * T] for a in range(n)]
                for a in range(n):
                    best = parts[a] if new else jnp.maximum(rows[r, :, a * T:(a + 1) * T], parts[a])
                    if not last:
                        rows[r, :, a * T:(a + 1) * T] = best
                        continue
                    for lo, size, start, who, key in segments:
                        add = row_sum(best[lo:lo + size], start, who)
                        sums[key, a] = plus(sums.get((key, a)), add)

            def catch_up():
                landed(k)
                x_side = right[k].reshape(2 * T, width)
                r = 2 * halves + k
                for j in range(k):
                    part = dot(x_side, left[j].reshape(2 * T, width))
                    for b in range(2):
                        cols[j, 2 + b] = jnp.maximum(cols[j, 2 + b], down(part[b * T:(b + 1) * T]))
                    rows[r] = part if j == 0 else jnp.maximum(rows[r], part)

            if others:
                catch_up()
            ready(k)
            y_side = left[k, :n].reshape(n * T, width)
            best = [None] * 4
            for b in range(2):
                for h in range(halves):
                    part = dot(own[b, 2 * T * h:2 * T * (h + 1)], y_side)
                    best[b] = fold(best[b], down(part))
                    meet(part, b * halves + h, k == 0, [(0, 2 * T, 2 * T * h, ours[b], ours_key(b))])
            if others:
                for j in range(k + 1):
                    part = dot(right[j].reshape(2 * T, width), y_side)
                    for b in range(2):
                        best[2 + b] = fold(best[2 + b], down(part[b * T:(b + 1) * T]))
                    meet(part, 2 * halves + j, k == 0,
                         [(b * T, T, j * T, others[b], 2 + b) for b in range(2)])
            for b in range(4 if others else 2):
                cols[k, b, :, :n * T] = best[b]
        whose = ours + list(others)
        table = jnp.zeros((slots, T), f32)
        for b in range(len(whose)):
            spread = jnp.zeros((8, T), f32)
            for a in range(n):
                spread = jnp.where(wide == ids[a], sums[b, a], spread)
            line = jnp.sum(spread, axis=0, keepdims=True) / length_of(whose[b]).astype(f32)
            table = jnp.where(high == whose[b], line, table)
        for a in range(n):
            stack = jnp.zeros((slots, T), f32)
            for b in range(len(whose)):
                across_sum = None
                for k in range(chunks):
                    across_sum = plus(across_sum, col_sum(cols[k, b, :, a * T:(a + 1) * T], k * T, ids[a]))
                stack = jnp.where(high == whose[b], across_sum, stack)
            totals = jnp.where(high == wide, jnp.sum(stack, axis=1, keepdims=True), f32(0.0))
            line = jnp.sum(totals, axis=0, keepdims=True) / length_of(ids[a]).astype(f32)
            table = jnp.where(high == ids[a], line, table)
        res[0] = table

    def ours_key(b):
        return b

    def arrived(k):
        copy(left.at[k, 0], left.at[k, 0], side_out, left_in.at[k], at(p, sib)).wait_recv()

    @pl.when(is_hub)
    def _():
        ids = [far, near]
        others = [end, end_other]

        def take(turns):
            for kind, m in turns:
                if kind == "on":
                    pass_on(m)
                else:
                    inward(m).wait_recv()
                    to_side(m).start()

        def steps(k):
            if k == 0:
                for i, who in enumerate(ids + others):
                    told(1 + i, who)
            take(turns(k))

        def landed(k):
            copy(right.at[k, 1], right.at[k, 1], right_out, side_in.at[k], at(p, sib)).wait_recv()

        def ready(k):
            arrived(k)
            copy(left.at[k, 1], left.at[k, 1], side_out, late_in.at[k], at(p, sib)).wait_recv()

        align(ids, others, ready, steps, landed)
        report(2, far).start()
        report(2, near).start()
        report(2, end).start()
        report(3, end_other).start()
        report(1, sib).start()

    @pl.when(is_far | is_end)
    def _():
        who = jnp.where(is_far, near, hub)

        def steps(k):
            if k == 0:
                told(1, who)

        @pl.when(is_far)
        def _():
            by_window(ahead_of, lambda window: paced(straight, AHEAD, count, window))

        @pl.when(is_end)
        def _():
            by_window(behind, lambda window: paced(inward, AHEAD, count, window))

        align([who], [], arrived, steps)
        report(1, sib).start()
        report(3, who).start()

    def reported(slot):
        copy(res.at[slot], res.at[slot], res_out, res_in.at[slot], at(p, sib)).wait_recv()

    @pl.when(is_near)
    def _():
        res[0] = jnp.zeros(res.shape[1:], f32)
        res[1] = jnp.zeros(res.shape[1:], f32)
        by_line(p, detour_sent)
        all_sent(side_out)
        small_sent(lens_out, 3)
        reported(3)
        reported(2)

    @pl.when(is_far)
    def _():
        res[3] = jnp.zeros(res.shape[1:], f32)
        by_window(ahead_of, lambda window: done(straight, window))
        small_sent(lens_out, 2)
        small_sent(res_out, 2)
        reported(1)
        reported(2)

    @pl.when(is_hub)
    def _():
        res[2] = jnp.zeros(res.shape[1:], f32)
        all_sent(side_out)
        all_sent(right_out)
        by_line(across, passed_on)
        small_sent(lens_out, 2)
        reported(3)
        reported(1)

    @pl.when(is_end)
    def _():
        by_window(behind, lambda window: done(inward, window))
        small_sent(lens_out, 3)
        small_sent(res_out, 2)
        for slot in range(1, 4):
            reported(slot)

    whole = pair[...] + res[0] + res[1] + res[2] + res[3]
    row = jnp.sum(jnp.where(high == s, whole, f32(0.0)), axis=0, keepdims=True)
    mine_too = ((high == s) | (wide == s)) & (high != wide)
    both = jnp.sum(jnp.where(mine_too, whole, f32(0.0)), axis=0, keepdims=True)
    score = jnp.sum(both, axis=1, keepdims=True) / f32(2 * (slots - 1))
    out_ref[...] = jnp.where(high == 0, row, score)
    share.wait_send()

    @pl.when(is_hub)
    def _():
        small_sent(res_out, 5)


def finish(found_ref, precision_ref, utility_ref):
    precision_ref[...] = found_ref[0:1, :precision_ref.shape[1]]
    utility_ref[...] = found_ref[1:2, 0:1]


def fused(slots, embeddings, lengths):
    length, width = embeddings.shape[1:]
    chunks = length // T
    count = max(len(pieces_of(length, direct)) for direct in DIRECT)
    many = length // PIECE
    dma = pltpu.SemaphoreType.DMA
    vmem = pl.BlockSpec(memory_space=pltpu.VMEM)
    away = pl.BlockSpec(memory_space=pl.ANY)
    found = pl.pallas_call(
        functools.partial(kernel, slots // 2, slots),
        out_shape=pltpu.VMEM((slots, T), jnp.float32),
        in_specs=[away, pl.BlockSpec(memory_space=pltpu.HBM)],
        out_specs=vmem,
        scratch_shapes=[
            pltpu.VMEM((chunks, T, width), jnp.bfloat16),
            pltpu.VMEM((2, length, width), jnp.bfloat16),
            pltpu.VMEM((chunks, 2, T, width), jnp.bfloat16),
            pltpu.VMEM((chunks, 2, T, width), jnp.bfloat16),
            pltpu.VMEM((length, width), jnp.bfloat16),
            pltpu.SMEM((1,), jnp.int32),
            pltpu.VMEM((slots, 8, T), jnp.int32),
            pltpu.VMEM((2 * chunks, 2 * T, 2 * T), jnp.float32),
            pltpu.VMEM((chunks, 4, 8, 2 * T), jnp.float32),
            pltpu.VMEM((slots, T), jnp.float32),
            pltpu.VMEM((4, slots, T), jnp.float32),
            dma((chunks + 1,)), dma((TURNS,)), dma(()), dma((2,)), dma(()), dma((chunks,)),
            dma((chunks,)), dma((count,)), dma((many,)), dma((chunks,)), dma(()),
            dma(()), dma((5,)), dma(()), dma((4,)),
        ],
        compiler_params=pltpu.CompilerParams(collective_id=0, has_side_effects=True),
    )(embeddings, lengths)
    precision, utility = pl.pallas_call(
        finish,
        out_shape=(jax.ShapeDtypeStruct((1, slots), jnp.float32), jax.ShapeDtypeStruct((1, 1), jnp.float32)),
        in_specs=[vmem],
        out_specs=(vmem, vmem),
    )(pltpu.with_memory_space_constraint(found, pltpu.VMEM))
    return precision, utility[:, 0]


def tile_pairs(own, own_len, other, other_len):
    similar = jnp.einsum("aie,bje->abij", own, other, preferred_element_type=jnp.float32)
    places = jnp.arange(own.shape[1], dtype=jnp.int32)
    own_ok = places[None, :] < own_len[:, None]
    other_ok = places[None, :] < other_len[:, None]
    masked = jnp.where(other_ok[None, :, None, :], similar, jnp.float32(-4.0))
    best_row = jnp.max(masked, axis=3)
    forward = jnp.sum(jnp.where(own_ok[:, None, :], best_row, jnp.float32(0.0)), axis=2)
    forward = forward / own_len[:, None].astype(jnp.float32)
    masked_col = jnp.where(own_ok[:, None, :, None], similar, jnp.float32(-4.0))
    best_col = jnp.max(masked_col, axis=2)
    backward = jnp.sum(jnp.where(other_ok[None, :, :], best_col, jnp.float32(0.0)), axis=2)
    backward = backward / other_len[None, :].astype(jnp.float32)
    return (forward, backward)


def body(embeddings, lengths):
    values = embeddings.astype(jnp.float32)
    unit = (values / jnp.sqrt(jnp.sum(values * values, axis=2, keepdims=True) + 1e-06)).astype(
        jnp.bfloat16
    )
    devices = lax.axis_size("sample")
    here = lax.axis_index("sample")
    per_dev = unit.shape[0]
    total = per_dev * devices
    base = here * per_dev
    piece = lax.all_gather(unit, "sample", axis=0, tiled=True)
    piece_len = lax.all_gather(lengths, "sample", axis=0, tiled=True)
    ahead, behind = tile_pairs(unit, lengths, piece, piece_len)
    own_index = base + jnp.arange(per_dev, dtype=jnp.int32)
    offdiag = jnp.arange(total, dtype=jnp.int32)[None, :] != own_index[:, None]
    utility = jnp.sum(jnp.where(offdiag, ahead + behind, jnp.float32(0.0)), axis=1)
    utility = utility / jnp.float32(2 * (total - 1))
    return (ahead, utility)


def solution(mesh):
    in_specs = (P(("prompt", "sample"), None, None), P(("prompt", "sample")))
    out_specs = (P(("prompt", "sample"), None), P(("prompt", "sample")))

    def run(embeddings, lengths):
        slots = mesh.shape["sample"]
        if mesh.shape["prompt"] == 4 and slots == 8 and embeddings.shape[0] == 1 and embeddings.shape[1] == 4 * T:
            return fused(slots, embeddings, lengths)
        return body(embeddings, lengths)

    return jax.shard_map(run, mesh=mesh, in_specs=in_specs, out_specs=out_specs, check_vma=False)
```

```python
import functools

import jax
import jax.numpy as jnp
from jax import lax
from jax.experimental import pallas as pl
from jax.experimental.pallas import tpu as pltpu
from jax.sharding import PartitionSpec as P

MESH = pl.DeviceIdType.MESH
T = 128
PIECE = 64
FIRST = (16, 16, 32)
DIRECT = (16, 48, 48, 64)
AHEAD = 2
MORE = 4
HOP = (4, 3, 3, 2)
WINDOW = (256, 192, 192, 128)
TURNS = 4


def pieces_of(length, direct):
    sizes = list(FIRST)
    while sum(sizes) < length - direct:
        sizes.append(min(PIECE, length - direct - sum(sizes)))
    return [(sum(sizes[:i]), n) for i, n in enumerate(sizes)]


def kernel(chips, slots, emb_ref, len_ref, out_ref, stage, own, left, right, relay, number, lens, rows, cols, pair, res,
           load, main_out, side_out, own_out, own_in, left_in, late_in, relay_in, right_in, side_in, right_out,
           lens_out, lens_in, res_out, res_in):
    p, s = lax.axis_index("prompt"), lax.axis_index("sample")
    x, y, z, c = p % 2, p // 2, s // 2, s % 2
    flip = (x + y) % 2
    v = jnp.where(flip == 0, z, chips - 1 - z)
    across = jnp.where(c == 0, p + 1 - 2 * x, p + 2 - 4 * y)
    length, width = own.shape[1:]
    chunks = length // T
    halves = length // (2 * T)
    plans = [pieces_of(length, direct) for direct in DIRECT]
    count = length // PIECE
    per = T // PIECE
    sib = 2 * z + 1 - c
    is_far, is_near, is_hub, is_end = v == 0, v == 1, v == 2, v == 3
    f32 = jnp.float32

    def sample(place, core):
        return 2 * jnp.where(flip == 0, place, chips - 1 - place) + core

    def at(prompt, who):
        return {"prompt": prompt, "sample": who}

    def copy(src, dst, out_sem, in_sem, where):
        return pltpu.make_async_remote_copy(
            src_ref=src, dst_ref=dst, send_sem=out_sem, recv_sem=in_sem,
            device_id=where, device_id_type=MESH)

    def chunk(k):
        return pl.ds(k * T, T)

    far, near, hub, end = (sample(i, c) for i in range(chips))
    hub_other, end_other = sample(2, 1 - c), sample(3, 1 - c)
    twin = at(across, 2 * (chips - 1 - z) + c)

    barrier = pltpu.get_barrier_semaphore()

    def greet(where):
        pl.semaphore_signal(barrier, inc=1, device_id=where, device_id_type=MESH)

    greet(at(p, sib))

    @pl.when(is_far)
    def _():
        greet(at(p, near))
        greet(at(p, hub))

    @pl.when(is_near)
    def _():
        greet(at(p, far))
        greet(at(p, hub))

    @pl.when(is_hub)
    def _():
        greet(at(across, s))
        greet(at(p, near))
        greet(at(p, far))
        greet(at(p, end))
        greet(at(p, end_other))
        greet(twin)

    @pl.when(is_end)
    def _():
        greet(at(p, hub))
        greet(at(p, hub_other))

    def fetch(k):
        n = 1 if k == 0 else chunks - 1
        return pltpu.make_async_copy(emb_ref.at[0, pl.ds(k * T, n * T)], stage.at[pl.ds(k * T, n * T)], load.at[k])

    fetch_len = pltpu.make_async_copy(len_ref, number, load.at[2])
    fetch_len.start()
    for k in range(2):
        fetch(k).start()
    fetch_len.wait()
    mine = number[0]
    lens[s] = jnp.full(lens.shape[1:], mine, jnp.int32)
    token = lax.broadcasted_iota(jnp.int32, (T, 1), 0)

    def scale(k, first):
        if k < 2:
            fetch(k).wait()
        values = stage[k * T:(k + 1) * T].astype(f32)
        unit = values * (1.0 / jnp.sqrt(jnp.sum(values * values, axis=1, keepdims=True) + 1e-06))
        first = unit[0:1] if first is None else first
        own[0, k * T:(k + 1) * T] = jnp.where(token + k * T < mine, unit, first).astype(own.dtype)
        return first

    lead = scale(0, None)

    def bit(m):
        return pl.ds(m * PIECE, PIECE)

    def spot(m):
        return pl.ds(m % per * PIECE, PIECE)

    def straight(m):
        return copy(own.at[0, bit(m)], left.at[m // per, 0, spot(m)], main_out.at[m % TURNS], left_in.at[m // per],
                    at(p, hub))

    def inward(m):
        return copy(own.at[0, bit(m)], right.at[m // per, 0, spot(m)], main_out.at[m % TURNS], right_in.at[m], at(p, hub))

    def detour(f, i):
        lo, n = plans[f][i]
        return copy(own.at[0, pl.ds(lo, n)], relay.at[pl.ds(lo, n)], main_out.at[i % TURNS], relay_in.at[i], at(across, s))

    def hand_on(f, i):
        lo, n = plans[f][i]
        return copy(relay.at[pl.ds(lo, n)], left.at[lo // T, 1, pl.ds(lo % T, n)], main_out.at[i % TURNS],
                    late_in.at[lo // T], twin)

    def shortcut(f):
        n = DIRECT[f]
        return copy(own.at[0, pl.ds(length - n, n)], left.at[chunks - 1, 1, pl.ds(T - n, n)],
                    own_out.at[1], late_in.at[chunks - 1], at(p, hub))

    def by_line(which, do):
        for f in range(len(DIRECT)):
            pl.when(which == f)(functools.partial(do, f))

    def outward(k, who):
        return copy(own.at[0, chunk(k)], left.at[k, 0], side_out, left_in.at[k], at(p, who))

    def to_side(m):
        return copy(right.at[m // per, 0, spot(m)], right.at[m // per, 1, spot(m)], right_out, side_in.at[m // per],
                    at(p, sib))

    def tell(i, who):
        return copy(lens.at[s], lens.at[s], lens_out, lens_in.at[i], at(p, who))

    def told(i, who):
        copy(lens.at[who], lens.at[who], lens_out, lens_in.at[i], at(p, sib)).wait_recv()

    def all_sent(sem):
        copy(own.at[0], own.at[0], sem, sem, at(p, sib)).wait_send()

    def small_sent(sem, n):
        copy(lens.at[pl.ds(0, n)], lens.at[pl.ds(0, n)], sem, sem, at(p, sib)).wait_send()

    def report(slot, who):
        return copy(res.at[0], res.at[slot], res_out, res_in.at[slot], at(p, who))

    share = copy(own.at[0], own.at[1], own_out.at[0], own_in, at(p, sib))

    def paced(send, lo, hi, ahead):
        for i in range(lo, hi):
            if i >= ahead:
                send(i - ahead).wait_send()
            send(i).start()

    def turns(k):
        return {
            0: [("in", 0), ("in", 1), ("on", 2), ("in", 2), ("on", 3)],
            1: [("in", 3), ("on", 4), ("in", 4), ("on", 5), ("in", 5), ("on", 6)],
            2: [("on", 7), ("in", 6)],
            3: [("in", 7)]}[k]

    def before(f, i):
        lo, n = plans[f][i]
        gone = [j for j, (start, size) in enumerate(plans[f][:i]) if start < lo + n - WINDOW[f] or j <= i - TURNS]
        return max(gone) if gone else -1

    def pass_on(m):
        def do(f):
            for i, (lo, n) in enumerate(plans[f]):
                if lo // PIECE == m:
                    part = relay.at[pl.ds(lo, n)]
                    copy(part, part, main_out.at[0], relay_in.at[i], twin).wait_recv()
                    for j in range(before(f, i - 1) + 1 if i else 0, before(f, i) + 1):
                        hand_on(f, j).wait_send()
                    hand_on(f, i).start()

        by_line(across, do)

    def passed_on(f):
        for i in range(before(f, len(plans[f]) - 1) + 1, len(plans[f])):
            hand_on(f, i).wait_send()

    def detour_rest(f):
        paced(functools.partial(detour, f), min(HOP), len(plans[f]), HOP[f])
        shortcut(f).start()

    def detour_sent(f):
        for i in range(len(plans[f]) - HOP[f], len(plans[f])):
            detour(f, i).wait_send()
        shortcut(f).wait_send()

    def done(send, window):
        for m in range(count - window, count):
            send(m).wait_send()

    def by_window(wider, do):
        pl.when(wider)(lambda: do(MORE))
        pl.when(jnp.logical_not(wider))(lambda: do(AHEAD))

    ahead_of = (p == 0) & (c == 0)
    behind = (p == 0) & (c == 1)

    @pl.when(is_far)
    def _():
        pl.semaphore_wait(barrier, 3)
        tell(1, hub).start()
        paced(straight, 0, AHEAD, AHEAD)

    @pl.when(is_near)
    def _():
        pl.semaphore_wait(barrier, 4)
        paced(functools.partial(detour, 0), 0, min(HOP), min(HOP))
        tell(2, hub).start()
        tell(1, far).start()

    @pl.when(is_hub)
    def _():
        pl.semaphore_wait(barrier, 6)
        tell(1, end).start()

    @pl.when(is_end)
    def _():
        pl.semaphore_wait(barrier, 3)
        tell(3, hub).start()
        tell(4, hub_other).start()
        paced(inward, 0, AHEAD, AHEAD)

    tell(0, sib).start()
    for k in range(1, chunks):
        scale(k, lead)
    share.start()

    @pl.when(is_near)
    def _():
        for k in range(chunks):
            outward(k, far).start()
        by_line(p, detour_rest)

    @pl.when(is_hub)
    def _():
        for k in range(chunks):
            outward(k, end).start()
        pass_on(0)
        pass_on(1)

    def dot(a, b):
        return lax.dot_general(a, b, (((1,), (1,)), ((), ())), preferred_element_type=f32)

    def fold(old, new):
        return new if old is None else jnp.maximum(old, new)

    def plus(old, new):
        return new if old is None else old + new

    def down(part):
        return jnp.max(part.reshape(part.shape[0] // 8, 8, part.shape[1]), axis=0)

    def length_of(who):
        return lens[who, 0:1, 0:1]

    def row_sum(best, start, who):
        top = jnp.max(best, axis=1, keepdims=True)
        place = lax.broadcasted_iota(jnp.int32, top.shape, 0) + start
        kept = jnp.where(place < length_of(who), top, f32(0.0))
        return jnp.sum(kept.reshape(top.shape[0] // 8, 8, 1), axis=0)

    def col_sum(best, start, who):
        top = jnp.max(best, axis=0, keepdims=True)
        place = lax.broadcasted_iota(jnp.int32, top.shape, 1) + start
        return jnp.where(place < length_of(who), top, f32(0.0))

    high = lax.broadcasted_iota(jnp.int32, (slots, T), 0)
    wide = lax.broadcasted_iota(jnp.int32, (slots, T), 1)

    def put(table, of, against, total):
        value = jnp.sum(jnp.sum(total, axis=0, keepdims=True), axis=1, keepdims=True)
        value = value / length_of(of).astype(f32)
        return jnp.where((high == of) & (wide == against), value, table)

    ours = [s, sib]
    share.wait_recv()
    told(0, sib)
    by_row = [None] * halves
    by_col = [None, None]
    for h in range(halves):
        y_side = own[0, 2 * T * h:2 * T * (h + 1)]
        best = [None, None]
        for b in range(2):
            for g in range(halves):
                part = dot(own[b, 2 * T * g:2 * T * (g + 1)], y_side)
                best[b] = fold(best[b], down(part))
                if b == 1:
                    by_row[g] = fold(by_row[g], jnp.maximum(part[:, :T], part[:, T:]))
        for b in range(2):
            by_col[b] = plus(by_col[b], col_sum(best[b], 2 * T * h, s))
    table = jnp.zeros((slots, T), f32)
    for b in range(2):
        table = put(table, s, ours[b], by_col[b])
    total = None
    for g in range(halves):
        total = plus(total, row_sum(by_row[g], 2 * T * g, sib))
    pair[...] = put(table, sib, s, total)

    def align(ids, others, ready, steps, landed=None):
        n = len(ids)
        sums = {}
        for k in range(chunks):
            last = k == chunks - 1
            steps(k)

            def meet(part, r, new, segments):
                parts = [part[:, a * T:(a + 1) * T] for a in range(n)]
                for a in range(n):
                    best = parts[a] if new else jnp.maximum(rows[r, :, a * T:(a + 1) * T], parts[a])
                    if not last:
                        rows[r, :, a * T:(a + 1) * T] = best
                        continue
                    for lo, size, start, who, key in segments:
                        add = row_sum(best[lo:lo + size], start, who)
                        sums[key, a] = plus(sums.get((key, a)), add)

            def catch_up():
                landed(k)
                x_side = right[k].reshape(2 * T, width)
                r = 2 * halves + k
                for j in range(k):
                    part = dot(x_side, left[j].reshape(2 * T, width))
                    for b in range(2):
                        cols[j, 2 + b] = jnp.maximum(cols[j, 2 + b], down(part[b * T:(b + 1) * T]))
                    rows[r] = part if j == 0 else jnp.maximum(rows[r], part)

            if others:
                catch_up()
            ready(k)
            y_side = left[k, :n].reshape(n * T, width)
            best = [None] * 4
            for b in range(2):
                for h in range(halves):
                    part = dot(own[b, 2 * T * h:2 * T * (h + 1)], y_side)
                    best[b] = fold(best[b], down(part))
                    meet(part, b * halves + h, k == 0, [(0, 2 * T, 2 * T * h, ours[b], ours_key(b))])
            if others:
                for j in range(k + 1):
                    part = dot(right[j].reshape(2 * T, width), y_side)
                    for b in range(2):
                        best[2 + b] = fold(best[2 + b], down(part[b * T:(b + 1) * T]))
                    meet(part, 2 * halves + j, k == 0,
                         [(b * T, T, j * T, others[b], 2 + b) for b in range(2)])
            for b in range(4 if others else 2):
                cols[k, b, :, :n * T] = best[b]
        whose = ours + list(others)
        table = jnp.zeros((slots, T), f32)
        for b in range(len(whose)):
            spread = jnp.zeros((8, T), f32)
            for a in range(n):
                spread = jnp.where(wide == ids[a], sums[b, a], spread)
            line = jnp.sum(spread, axis=0, keepdims=True) / length_of(whose[b]).astype(f32)
            table = jnp.where(high == whose[b], line, table)
        for a in range(n):
            stack = jnp.zeros((slots, T), f32)
            for b in range(len(whose)):
                across_sum = None
                for k in range(chunks):
                    across_sum = plus(across_sum, col_sum(cols[k, b, :, a * T:(a + 1) * T], k * T, ids[a]))
                stack = jnp.where(high == whose[b], across_sum, stack)
            totals = jnp.where(high == wide, jnp.sum(stack, axis=1, keepdims=True), f32(0.0))
            line = jnp.sum(totals, axis=0, keepdims=True) / length_of(ids[a]).astype(f32)
            table = jnp.where(high == ids[a], line, table)
        res[0] = table

    def ours_key(b):
        return b

    def arrived(k):
        copy(left.at[k, 0], left.at[k, 0], side_out, left_in.at[k], at(p, sib)).wait_recv()

    @pl.when(is_hub)
    def _():
        ids = [far, near]
        others = [end, end_other]

        def take(turns):
            for kind, m in turns:
                if kind == "on":
                    pass_on(m)
                else:
                    inward(m).wait_recv()
                    to_side(m).start()

        def steps(k):
            if k == 0:
                for i, who in enumerate(ids + others):
                    told(1 + i, who)
            take(turns(k))

        def landed(k):
            copy(right.at[k, 1], right.at[k, 1], right_out, side_in.at[k], at(p, sib)).wait_recv()

        def ready(k):
            arrived(k)
            copy(left.at[k, 1], left.at[k, 1], side_out, late_in.at[k], at(p, sib)).wait_recv()

        align(ids, others, ready, steps, landed)
        report(2, far).start()
        report(2, near).start()
        report(2, end).start()
        report(3, end_other).start()
        report(1, sib).start()

    @pl.when(is_far | is_end)
    def _():
        who = jnp.where(is_far, near, hub)

        def steps(k):
            if k == 0:
                told(1, who)

        @pl.when(is_far)
        def _():
            by_window(ahead_of, lambda window: paced(straight, AHEAD, count, window))

        @pl.when(is_end)
        def _():
            by_window(behind, lambda window: paced(inward, AHEAD, count, window))

        align([who], [], arrived, steps)
        report(1, sib).start()
        report(3, who).start()

    def reported(slot):
        copy(res.at[slot], res.at[slot], res_out, res_in.at[slot], at(p, sib)).wait_recv()

    @pl.when(is_near)
    def _():
        res[0] = jnp.zeros(res.shape[1:], f32)
        res[1] = jnp.zeros(res.shape[1:], f32)
        by_line(p, detour_sent)
        all_sent(side_out)
        small_sent(lens_out, 3)
        reported(3)
        reported(2)

    @pl.when(is_far)
    def _():
        res[3] = jnp.zeros(res.shape[1:], f32)
        by_window(ahead_of, lambda window: done(straight, window))
        small_sent(lens_out, 2)
        small_sent(res_out, 2)
        reported(1)
        reported(2)

    @pl.when(is_hub)
    def _():
        res[2] = jnp.zeros(res.shape[1:], f32)
        all_sent(side_out)
        all_sent(right_out)
        by_line(across, passed_on)
        small_sent(lens_out, 2)
        reported(3)
        reported(1)

    @pl.when(is_end)
    def _():
        by_window(behind, lambda window: done(inward, window))
        small_sent(lens_out, 3)
        small_sent(res_out, 2)
        for slot in range(1, 4):
            reported(slot)

    whole = pair[...] + res[0] + res[1] + res[2] + res[3]
    row = jnp.sum(jnp.where(high == s, whole, f32(0.0)), axis=0, keepdims=True)
    mine_too = ((high == s) | (wide == s)) & (high != wide)
    both = jnp.sum(jnp.where(mine_too, whole, f32(0.0)), axis=0, keepdims=True)
    score = jnp.sum(both, axis=1, keepdims=True) / f32(2 * (slots - 1))
    out_ref[...] = jnp.where(high == 0, row, score)
    share.wait_send()

    @pl.when(is_hub)
    def _():
        small_sent(res_out, 5)


def finish(found_ref, precision_ref, utility_ref):
    precision_ref[...] = found_ref[0:1, :precision_ref.shape[1]]
    utility_ref[...] = found_ref[1:2, 0:1]


def fused(slots, embeddings, lengths):
    length, width = embeddings.shape[1:]
    chunks = length // T
    count = max(len(pieces_of(length, direct)) for direct in DIRECT)
    many = length // PIECE
    dma = pltpu.SemaphoreType.DMA
    vmem = pl.BlockSpec(memory_space=pltpu.VMEM)
    away = pl.BlockSpec(memory_space=pl.ANY)
    found = pl.pallas_call(
        functools.partial(kernel, slots // 2, slots),
        out_shape=pltpu.VMEM((slots, T), jnp.float32),
        in_specs=[away, pl.BlockSpec(memory_space=pltpu.HBM)],
        out_specs=vmem,
        scratch_shapes=[
            pltpu.VMEM((length, width), jnp.bfloat16),
            pltpu.VMEM((2, length, width), jnp.bfloat16),
            pltpu.VMEM((chunks, 2, T, width), jnp.bfloat16),
            pltpu.VMEM((chunks, 2, T, width), jnp.bfloat16),
            pltpu.VMEM((length, width), jnp.bfloat16),
            pltpu.SMEM((1,), jnp.int32),
            pltpu.VMEM((slots, 8, T), jnp.int32),
            pltpu.VMEM((2 * chunks, 2 * T, 2 * T), jnp.float32),
            pltpu.VMEM((chunks, 4, 8, 2 * T), jnp.float32),
            pltpu.VMEM((slots, T), jnp.float32),
            pltpu.VMEM((4, slots, T), jnp.float32),
            dma((3,)), dma((TURNS,)), dma(()), dma((2,)), dma(()), dma((chunks,)),
            dma((chunks,)), dma((count,)), dma((many,)), dma((chunks,)), dma(()),
            dma(()), dma((5,)), dma(()), dma((4,)),
        ],
        compiler_params=pltpu.CompilerParams(collective_id=0, has_side_effects=True),
    )(embeddings, lengths)
    precision, utility = pl.pallas_call(
        finish,
        out_shape=(jax.ShapeDtypeStruct((1, slots), jnp.float32), jax.ShapeDtypeStruct((1, 1), jnp.float32)),
        in_specs=[vmem],
        out_specs=(vmem, vmem),
    )(pltpu.with_memory_space_constraint(found, pltpu.VMEM))
    return precision, utility[:, 0]


def tile_pairs(own, own_len, other, other_len):
    similar = jnp.einsum("aie,bje->abij", own, other, preferred_element_type=jnp.float32)
    places = jnp.arange(own.shape[1], dtype=jnp.int32)
    own_ok = places[None, :] < own_len[:, None]
    other_ok = places[None, :] < other_len[:, None]
    masked = jnp.where(other_ok[None, :, None, :], similar, jnp.float32(-4.0))
    best_row = jnp.max(masked, axis=3)
    forward = jnp.sum(jnp.where(own_ok[:, None, :], best_row, jnp.float32(0.0)), axis=2)
    forward = forward / own_len[:, None].astype(jnp.float32)
    masked_col = jnp.where(own_ok[:, None, :, None], similar, jnp.float32(-4.0))
    best_col = jnp.max(masked_col, axis=2)
    backward = jnp.sum(jnp.where(other_ok[None, :, :], best_col, jnp.float32(0.0)), axis=2)
    backward = backward / other_len[None, :].astype(jnp.float32)
    return (forward, backward)


def body(embeddings, lengths):
    values = embeddings.astype(jnp.float32)
    unit = (values / jnp.sqrt(jnp.sum(values * values, axis=2, keepdims=True) + 1e-06)).astype(
        jnp.bfloat16
    )
    devices = lax.axis_size("sample")
    here = lax.axis_index("sample")
    per_dev = unit.shape[0]
    total = per_dev * devices
    base = here * per_dev
    piece = lax.all_gather(unit, "sample", axis=0, tiled=True)
    piece_len = lax.all_gather(lengths, "sample", axis=0, tiled=True)
    ahead, behind = tile_pairs(unit, lengths, piece, piece_len)
    own_index = base + jnp.arange(per_dev, dtype=jnp.int32)
    offdiag = jnp.arange(total, dtype=jnp.int32)[None, :] != own_index[:, None]
    utility = jnp.sum(jnp.where(offdiag, ahead + behind, jnp.float32(0.0)), axis=1)
    utility = utility / jnp.float32(2 * (total - 1))
    return (ahead, utility)


def solution(mesh):
    in_specs = (P(("prompt", "sample"), None, None), P(("prompt", "sample")))
    out_specs = (P(("prompt", "sample"), None), P(("prompt", "sample")))

    def run(embeddings, lengths):
        slots = mesh.shape["sample"]
        if mesh.shape["prompt"] == 4 and slots == 8 and embeddings.shape[0] == 1 and embeddings.shape[1] == 4 * T:
            return fused(slots, embeddings, lengths)
        return body(embeddings, lengths)

    return jax.shard_map(run, mesh=mesh, in_specs=in_specs, out_specs=out_specs, check_vma=False)
```

```python
import functools

import jax
import jax.numpy as jnp
from jax import lax
from jax.experimental import pallas as pl
from jax.experimental.pallas import tpu as pltpu
from jax.sharding import PartitionSpec as P

MESH = pl.DeviceIdType.MESH
T = 128
PIECE = 64
FIRST = (16, 48)
DIRECT = (32, 48, 48, 48)
AHEAD = 2
MORE = 3
HOP = (3, 3, 3, 3)
WINDOW = (256, 192, 192, 128)
TURNS = 4


def pieces_of(length, direct):
    sizes = list(FIRST)
    while sum(sizes) < length - direct:
        sizes.append(min(PIECE, length - direct - sum(sizes)))
    return [(sum(sizes[:i]), n) for i, n in enumerate(sizes)]


def kernel(chips, slots, emb_ref, len_ref, out_ref, stage, own, left, right, relay, number, lens, rows, cols, pair, res,
           load, main_out, side_out, own_out, own_in, left_in, late_in, relay_in, right_in, side_in, right_out,
           lens_out, lens_in, res_out, res_in):
    p, s = lax.axis_index("prompt"), lax.axis_index("sample")
    x, y, z, c = p % 2, p // 2, s // 2, s % 2
    flip = (x + y) % 2
    v = jnp.where(flip == 0, z, chips - 1 - z)
    across = jnp.where(c == 0, p + 1 - 2 * x, p + 2 - 4 * y)
    length, width = own.shape[1:]
    chunks = length // T
    halves = length // (2 * T)
    plans = [pieces_of(length, direct) for direct in DIRECT]
    count = length // PIECE
    per = T // PIECE
    sib = 2 * z + 1 - c
    is_far, is_near, is_hub, is_end = v == 0, v == 1, v == 2, v == 3
    f32 = jnp.float32

    def sample(place, core):
        return 2 * jnp.where(flip == 0, place, chips - 1 - place) + core

    def at(prompt, who):
        return {"prompt": prompt, "sample": who}

    def copy(src, dst, out_sem, in_sem, where):
        return pltpu.make_async_remote_copy(
            src_ref=src, dst_ref=dst, send_sem=out_sem, recv_sem=in_sem,
            device_id=where, device_id_type=MESH)

    def chunk(k):
        return pl.ds(k * T, T)

    far, near, hub, end = (sample(i, c) for i in range(chips))
    hub_other, end_other = sample(2, 1 - c), sample(3, 1 - c)
    twin = at(across, 2 * (chips - 1 - z) + c)

    barrier = pltpu.get_barrier_semaphore()

    def greet(where):
        pl.semaphore_signal(barrier, inc=1, device_id=where, device_id_type=MESH)

    greet(at(p, sib))

    @pl.when(is_far)
    def _():
        greet(at(p, near))
        greet(at(p, hub))

    @pl.when(is_near)
    def _():
        greet(at(p, far))
        greet(at(p, hub))

    @pl.when(is_hub)
    def _():
        greet(at(across, s))
        greet(at(p, near))
        greet(at(p, far))
        greet(at(p, end))
        greet(at(p, end_other))
        greet(twin)

    @pl.when(is_end)
    def _():
        greet(at(p, hub))
        greet(at(p, hub_other))

    def fetch(k):
        n = 1 if k == 0 else chunks - 1
        return pltpu.make_async_copy(emb_ref.at[0, pl.ds(k * T, n * T)], stage.at[pl.ds(k * T, n * T)], load.at[k])

    fetch_len = pltpu.make_async_copy(len_ref, number, load.at[2])
    fetch_len.start()
    for k in range(2):
        fetch(k).start()
    fetch_len.wait()
    mine = number[0]
    lens[s] = jnp.full(lens.shape[1:], mine, jnp.int32)
    token = lax.broadcasted_iota(jnp.int32, (T, 1), 0)

    def scale(k, first):
        if k < 2:
            fetch(k).wait()
        values = stage[k * T:(k + 1) * T].astype(f32)
        unit = values * (1.0 / jnp.sqrt(jnp.sum(values * values, axis=1, keepdims=True) + 1e-06))
        first = unit[0:1] if first is None else first
        own[0, k * T:(k + 1) * T] = jnp.where(token + k * T < mine, unit, first).astype(own.dtype)
        return first

    lead = scale(0, None)

    def bit(m):
        return pl.ds(m * PIECE, PIECE)

    def spot(m):
        return pl.ds(m % per * PIECE, PIECE)

    def straight(m):
        return copy(own.at[0, bit(m)], left.at[m // per, 0, spot(m)], main_out.at[m % TURNS], left_in.at[m // per],
                    at(p, hub))

    def inward(m):
        return copy(own.at[0, bit(m)], right.at[m // per, 0, spot(m)], main_out.at[m % TURNS], right_in.at[m], at(p, hub))

    def detour(f, i):
        lo, n = plans[f][i]
        return copy(own.at[0, pl.ds(lo, n)], relay.at[pl.ds(lo, n)], main_out.at[i % TURNS], relay_in.at[i], at(across, s))

    def hand_on(f, i):
        lo, n = plans[f][i]
        return copy(relay.at[pl.ds(lo, n)], left.at[lo // T, 1, pl.ds(lo % T, n)], main_out.at[i % TURNS],
                    late_in.at[lo // T], twin)

    def shortcut(f):
        n = DIRECT[f]
        return copy(own.at[0, pl.ds(length - n, n)], left.at[chunks - 1, 1, pl.ds(T - n, n)],
                    own_out.at[1], late_in.at[chunks - 1], at(p, hub))

    def by_line(which, do):
        for f in range(len(DIRECT)):
            pl.when(which == f)(functools.partial(do, f))

    def outward(k, who):
        return copy(own.at[0, chunk(k)], left.at[k, 0], side_out, left_in.at[k], at(p, who))

    def to_side(m):
        return copy(right.at[m // per, 0, spot(m)], right.at[m // per, 1, spot(m)], right_out, side_in.at[m // per],
                    at(p, sib))

    def tell(i, who):
        return copy(lens.at[s], lens.at[s], lens_out, lens_in.at[i], at(p, who))

    def told(i, who):
        copy(lens.at[who], lens.at[who], lens_out, lens_in.at[i], at(p, sib)).wait_recv()

    def all_sent(sem):
        copy(own.at[0], own.at[0], sem, sem, at(p, sib)).wait_send()

    def small_sent(sem, n):
        copy(lens.at[pl.ds(0, n)], lens.at[pl.ds(0, n)], sem, sem, at(p, sib)).wait_send()

    def report(slot, who):
        return copy(res.at[0], res.at[slot], res_out, res_in.at[slot], at(p, who))

    share = copy(own.at[0], own.at[1], own_out.at[0], own_in, at(p, sib))

    def paced(send, lo, hi, ahead):
        for i in range(lo, hi):
            if i >= ahead:
                send(i - ahead).wait_send()
            send(i).start()

    def turns(k):
        return {
            0: [("in", 0), ("in", 1), ("on", 2), ("in", 2), ("on", 3)],
            1: [("in", 3), ("on", 4), ("in", 4), ("on", 5), ("in", 5), ("on", 6)],
            2: [("on", 7), ("in", 6)],
            3: [("in", 7)]}[k]

    def before(f, i):
        lo, n = plans[f][i]
        gone = [j for j, (start, size) in enumerate(plans[f][:i]) if start < lo + n - WINDOW[f] or j <= i - TURNS]
        return max(gone) if gone else -1

    def pass_on(m):
        def do(f):
            for i, (lo, n) in enumerate(plans[f]):
                if lo // PIECE == m:
                    part = relay.at[pl.ds(lo, n)]
                    copy(part, part, main_out.at[0], relay_in.at[i], twin).wait_recv()
                    for j in range(before(f, i - 1) + 1 if i else 0, before(f, i) + 1):
                        hand_on(f, j).wait_send()
                    hand_on(f, i).start()

        by_line(across, do)

    def passed_on(f):
        for i in range(before(f, len(plans[f]) - 1) + 1, len(plans[f])):
            hand_on(f, i).wait_send()

    def detour_rest(f):
        paced(functools.partial(detour, f), min(HOP), len(plans[f]), HOP[f])
        shortcut(f).start()

    def detour_sent(f):
        for i in range(len(plans[f]) - HOP[f], len(plans[f])):
            detour(f, i).wait_send()
        shortcut(f).wait_send()

    def done(send, window):
        for m in range(count - window, count):
            send(m).wait_send()

    def by_window(wider, do):
        pl.when(wider)(lambda: do(MORE))
        pl.when(jnp.logical_not(wider))(lambda: do(AHEAD))

    ahead_of = (p == 0) & (c == 0)
    behind = (p == 0) & (c == 1)

    @pl.when(is_far)
    def _():
        pl.semaphore_wait(barrier, 3)
        tell(1, hub).start()
        paced(straight, 0, AHEAD, AHEAD)

    @pl.when(is_near)
    def _():
        pl.semaphore_wait(barrier, 4)
        paced(functools.partial(detour, 0), 0, min(HOP), min(HOP))
        tell(2, hub).start()
        tell(1, far).start()

    @pl.when(is_hub)
    def _():
        pl.semaphore_wait(barrier, 6)
        tell(1, end).start()

    @pl.when(is_end)
    def _():
        pl.semaphore_wait(barrier, 3)
        tell(3, hub).start()
        tell(4, hub_other).start()
        paced(inward, 0, AHEAD, AHEAD)

    tell(0, sib).start()
    for k in range(1, chunks):
        scale(k, lead)
    share.start()

    @pl.when(is_near)
    def _():
        for k in range(chunks):
            outward(k, far).start()
        by_line(p, detour_rest)

    @pl.when(is_hub)
    def _():
        for k in range(chunks):
            outward(k, end).start()
        pass_on(0)
        pass_on(1)

    def dot(a, b):
        return lax.dot_general(a, b, (((1,), (1,)), ((), ())), preferred_element_type=f32)

    def fold(old, new):
        return new if old is None else jnp.maximum(old, new)

    def plus(old, new):
        return new if old is None else old + new

    def down(part):
        return jnp.max(part.reshape(part.shape[0] // 8, 8, part.shape[1]), axis=0)

    def length_of(who):
        return lens[who, 0:1, 0:1]

    def row_sum(best, start, who):
        top = jnp.max(best, axis=1, keepdims=True)
        place = lax.broadcasted_iota(jnp.int32, top.shape, 0) + start
        kept = jnp.where(place < length_of(who), top, f32(0.0))
        return jnp.sum(kept.reshape(top.shape[0] // 8, 8, 1), axis=0)

    def col_sum(best, start, who):
        top = jnp.max(best, axis=0, keepdims=True)
        place = lax.broadcasted_iota(jnp.int32, top.shape, 1) + start
        return jnp.where(place < length_of(who), top, f32(0.0))

    high = lax.broadcasted_iota(jnp.int32, (slots, T), 0)
    wide = lax.broadcasted_iota(jnp.int32, (slots, T), 1)

    def put(table, of, against, total):
        value = jnp.sum(jnp.sum(total, axis=0, keepdims=True), axis=1, keepdims=True)
        value = value / length_of(of).astype(f32)
        return jnp.where((high == of) & (wide == against), value, table)

    ours = [s, sib]
    share.wait_recv()
    told(0, sib)
    by_row = [None] * halves
    by_col = [None, None]
    for h in range(halves):
        y_side = own[0, 2 * T * h:2 * T * (h + 1)]
        best = [None, None]
        for b in range(2):
            for g in range(halves):
                part = dot(own[b, 2 * T * g:2 * T * (g + 1)], y_side)
                best[b] = fold(best[b], down(part))
                if b == 1:
                    by_row[g] = fold(by_row[g], jnp.maximum(part[:, :T], part[:, T:]))
        for b in range(2):
            by_col[b] = plus(by_col[b], col_sum(best[b], 2 * T * h, s))
    table = jnp.zeros((slots, T), f32)
    for b in range(2):
        table = put(table, s, ours[b], by_col[b])
    total = None
    for g in range(halves):
        total = plus(total, row_sum(by_row[g], 2 * T * g, sib))
    pair[...] = put(table, sib, s, total)

    def align(ids, others, ready, steps, landed=None):
        n = len(ids)
        sums = {}
        for k in range(chunks):
            last = k == chunks - 1
            steps(k)

            def meet(part, r, new, segments):
                parts = [part[:, a * T:(a + 1) * T] for a in range(n)]
                for a in range(n):
                    best = parts[a] if new else jnp.maximum(rows[r, :, a * T:(a + 1) * T], parts[a])
                    if not last:
                        rows[r, :, a * T:(a + 1) * T] = best
                        continue
                    for lo, size, start, who, key in segments:
                        add = row_sum(best[lo:lo + size], start, who)
                        sums[key, a] = plus(sums.get((key, a)), add)

            def catch_up():
                landed(k)
                x_side = right[k].reshape(2 * T, width)
                r = 2 * halves + k
                for j in range(k):
                    part = dot(x_side, left[j].reshape(2 * T, width))
                    for b in range(2):
                        cols[j, 2 + b] = jnp.maximum(cols[j, 2 + b], down(part[b * T:(b + 1) * T]))
                    rows[r] = part if j == 0 else jnp.maximum(rows[r], part)

            if others:
                catch_up()
            ready(k)
            y_side = left[k, :n].reshape(n * T, width)
            best = [None] * 4
            for b in range(2):
                for h in range(halves):
                    part = dot(own[b, 2 * T * h:2 * T * (h + 1)], y_side)
                    best[b] = fold(best[b], down(part))
                    meet(part, b * halves + h, k == 0, [(0, 2 * T, 2 * T * h, ours[b], ours_key(b))])
            if others:
                for j in range(k + 1):
                    part = dot(right[j].reshape(2 * T, width), y_side)
                    for b in range(2):
                        best[2 + b] = fold(best[2 + b], down(part[b * T:(b + 1) * T]))
                    meet(part, 2 * halves + j, k == 0,
                         [(b * T, T, j * T, others[b], 2 + b) for b in range(2)])
            for b in range(4 if others else 2):
                cols[k, b, :, :n * T] = best[b]
        whose = ours + list(others)
        table = jnp.zeros((slots, T), f32)
        for b in range(len(whose)):
            spread = jnp.zeros((8, T), f32)
            for a in range(n):
                spread = jnp.where(wide == ids[a], sums[b, a], spread)
            line = jnp.sum(spread, axis=0, keepdims=True) / length_of(whose[b]).astype(f32)
            table = jnp.where(high == whose[b], line, table)
        for a in range(n):
            stack = jnp.zeros((slots, T), f32)
            for b in range(len(whose)):
                across_sum = None
                for k in range(chunks):
                    across_sum = plus(across_sum, col_sum(cols[k, b, :, a * T:(a + 1) * T], k * T, ids[a]))
                stack = jnp.where(high == whose[b], across_sum, stack)
            totals = jnp.where(high == wide, jnp.sum(stack, axis=1, keepdims=True), f32(0.0))
            line = jnp.sum(totals, axis=0, keepdims=True) / length_of(ids[a]).astype(f32)
            table = jnp.where(high == ids[a], line, table)
        res[0] = table

    def ours_key(b):
        return b

    def arrived(k):
        copy(left.at[k, 0], left.at[k, 0], side_out, left_in.at[k], at(p, sib)).wait_recv()

    @pl.when(is_hub)
    def _():
        ids = [far, near]
        others = [end, end_other]

        def take(turns):
            for kind, m in turns:
                if kind == "on":
                    pass_on(m)
                else:
                    inward(m).wait_recv()
                    to_side(m).start()

        def steps(k):
            if k == 0:
                for i, who in enumerate(ids + others):
                    told(1 + i, who)
            take(turns(k))

        def landed(k):
            copy(right.at[k, 1], right.at[k, 1], right_out, side_in.at[k], at(p, sib)).wait_recv()

        def ready(k):
            arrived(k)
            copy(left.at[k, 1], left.at[k, 1], side_out, late_in.at[k], at(p, sib)).wait_recv()

        align(ids, others, ready, steps, landed)
        report(2, far).start()
        report(2, near).start()
        report(2, end).start()
        report(3, end_other).start()
        report(1, sib).start()

    @pl.when(is_far | is_end)
    def _():
        who = jnp.where(is_far, near, hub)

        def steps(k):
            if k == 0:
                told(1, who)

        @pl.when(is_far)
        def _():
            by_window(ahead_of, lambda window: paced(straight, AHEAD, count, window))

        @pl.when(is_end)
        def _():
            by_window(behind, lambda window: paced(inward, AHEAD, count, window))

        align([who], [], arrived, steps)
        report(1, sib).start()
        report(3, who).start()

    def reported(slot):
        copy(res.at[slot], res.at[slot], res_out, res_in.at[slot], at(p, sib)).wait_recv()

    @pl.when(is_near)
    def _():
        res[0] = jnp.zeros(res.shape[1:], f32)
        res[1] = jnp.zeros(res.shape[1:], f32)
        by_line(p, detour_sent)
        all_sent(side_out)
        small_sent(lens_out, 3)
        reported(3)
        reported(2)

    @pl.when(is_far)
    def _():
        res[3] = jnp.zeros(res.shape[1:], f32)
        by_window(ahead_of, lambda window: done(straight, window))
        small_sent(lens_out, 2)
        small_sent(res_out, 2)
        reported(1)
        reported(2)

    @pl.when(is_hub)
    def _():
        res[2] = jnp.zeros(res.shape[1:], f32)
        all_sent(side_out)
        all_sent(right_out)
        by_line(across, passed_on)
        small_sent(lens_out, 2)
        reported(3)
        reported(1)

    @pl.when(is_end)
    def _():
        by_window(behind, lambda window: done(inward, window))
        small_sent(lens_out, 3)
        small_sent(res_out, 2)
        for slot in range(1, 4):
            reported(slot)

    whole = pair[...] + res[0] + res[1] + res[2] + res[3]
    row = jnp.sum(jnp.where(high == s, whole, f32(0.0)), axis=0, keepdims=True)
    mine_too = ((high == s) | (wide == s)) & (high != wide)
    both = jnp.sum(jnp.where(mine_too, whole, f32(0.0)), axis=0, keepdims=True)
    score = jnp.sum(both, axis=1, keepdims=True) / f32(2 * (slots - 1))
    out_ref[...] = jnp.where(high == 0, row, score)
    share.wait_send()

    @pl.when(is_hub)
    def _():
        small_sent(res_out, 5)


def finish(found_ref, precision_ref, utility_ref):
    precision_ref[...] = found_ref[0:1, :precision_ref.shape[1]]
    utility_ref[...] = found_ref[1:2, 0:1]


def fused(slots, embeddings, lengths):
    length, width = embeddings.shape[1:]
    chunks = length // T
    count = max(len(pieces_of(length, direct)) for direct in DIRECT)
    many = length // PIECE
    dma = pltpu.SemaphoreType.DMA
    vmem = pl.BlockSpec(memory_space=pltpu.VMEM)
    away = pl.BlockSpec(memory_space=pl.ANY)
    found = pl.pallas_call(
        functools.partial(kernel, slots // 2, slots),
        out_shape=pltpu.VMEM((slots, T), jnp.float32),
        in_specs=[away, pl.BlockSpec(memory_space=pltpu.HBM)],
        out_specs=vmem,
        scratch_shapes=[
            pltpu.VMEM((length, width), jnp.bfloat16),
            pltpu.VMEM((2, length, width), jnp.bfloat16),
            pltpu.VMEM((chunks, 2, T, width), jnp.bfloat16),
            pltpu.VMEM((chunks, 2, T, width), jnp.bfloat16),
            pltpu.VMEM((length, width), jnp.bfloat16),
            pltpu.SMEM((1,), jnp.int32),
            pltpu.VMEM((slots, 8, T), jnp.int32),
            pltpu.VMEM((2 * chunks, 2 * T, 2 * T), jnp.float32),
            pltpu.VMEM((chunks, 4, 8, 2 * T), jnp.float32),
            pltpu.VMEM((slots, T), jnp.float32),
            pltpu.VMEM((4, slots, T), jnp.float32),
            dma((3,)), dma((TURNS,)), dma(()), dma((2,)), dma(()), dma((chunks,)),
            dma((chunks,)), dma((count,)), dma((many,)), dma((chunks,)), dma(()),
            dma(()), dma((5,)), dma(()), dma((4,)),
        ],
        compiler_params=pltpu.CompilerParams(collective_id=0, has_side_effects=True),
    )(embeddings, lengths)
    precision, utility = pl.pallas_call(
        finish,
        out_shape=(jax.ShapeDtypeStruct((1, slots), jnp.float32), jax.ShapeDtypeStruct((1, 1), jnp.float32)),
        in_specs=[vmem],
        out_specs=(vmem, vmem),
    )(pltpu.with_memory_space_constraint(found, pltpu.VMEM))
    return precision, utility[:, 0]


def tile_pairs(own, own_len, other, other_len):
    similar = jnp.einsum("aie,bje->abij", own, other, preferred_element_type=jnp.float32)
    places = jnp.arange(own.shape[1], dtype=jnp.int32)
    own_ok = places[None, :] < own_len[:, None]
    other_ok = places[None, :] < other_len[:, None]
    masked = jnp.where(other_ok[None, :, None, :], similar, jnp.float32(-4.0))
    best_row = jnp.max(masked, axis=3)
    forward = jnp.sum(jnp.where(own_ok[:, None, :], best_row, jnp.float32(0.0)), axis=2)
    forward = forward / own_len[:, None].astype(jnp.float32)
    masked_col = jnp.where(own_ok[:, None, :, None], similar, jnp.float32(-4.0))
    best_col = jnp.max(masked_col, axis=2)
    backward = jnp.sum(jnp.where(other_ok[None, :, :], best_col, jnp.float32(0.0)), axis=2)
    backward = backward / other_len[None, :].astype(jnp.float32)
    return (forward, backward)


def body(embeddings, lengths):
    values = embeddings.astype(jnp.float32)
    unit = (values / jnp.sqrt(jnp.sum(values * values, axis=2, keepdims=True) + 1e-06)).astype(
        jnp.bfloat16
    )
    devices = lax.axis_size("sample")
    here = lax.axis_index("sample")
    per_dev = unit.shape[0]
    total = per_dev * devices
    base = here * per_dev
    piece = lax.all_gather(unit, "sample", axis=0, tiled=True)
    piece_len = lax.all_gather(lengths, "sample", axis=0, tiled=True)
    ahead, behind = tile_pairs(unit, lengths, piece, piece_len)
    own_index = base + jnp.arange(per_dev, dtype=jnp.int32)
    offdiag = jnp.arange(total, dtype=jnp.int32)[None, :] != own_index[:, None]
    utility = jnp.sum(jnp.where(offdiag, ahead + behind, jnp.float32(0.0)), axis=1)
    utility = utility / jnp.float32(2 * (total - 1))
    return (ahead, utility)


def solution(mesh):
    in_specs = (P(("prompt", "sample"), None, None), P(("prompt", "sample")))
    out_specs = (P(("prompt", "sample"), None), P(("prompt", "sample")))

    def run(embeddings, lengths):
        slots = mesh.shape["sample"]
        if mesh.shape["prompt"] == 4 and slots == 8 and embeddings.shape[0] == 1 and embeddings.shape[1] == 4 * T:
            return fused(slots, embeddings, lengths)
        return body(embeddings, lengths)

    return jax.shard_map(run, mesh=mesh, in_specs=in_specs, out_specs=out_specs, check_vma=False)
```
